128 devices in a mesh: px: 16 (over y, x), py: 8 (over z, core).
Axes of the slice: x: 4, y: 4, z: 4, core: 2. Of those that a mesh axis runs over, the one named last changes fastest.
Arguments:
- fields: bfloat16 [4, 16, 1024, 1024], P(None, None, 'px', 'py'), may hold values from -6 to 6
- x_operators: bfloat16 [3, 1024, 1024], replicated
- y_operators: bfloat16 [3, 1024, 1024], replicated
- viscosity: float32 [4], replicated, may hold values from 0.1 to 1
- wall_tile: int32 [16384], P(('px', 'py')), may hold values from 0 to 1023
- wall_owner: int32 [16384, 1], P(('px', 'py')), may hold values from 0 to 127; in each aligned block of 128 rows (0 to 127, 128 to 255, ...) at most 4 rows name the same one
- wall_row: int32 [16384], P(('px', 'py')), may hold values from 0 to 63
- solid_temp: float32 [1024, 1024], P('px', 'py'), may hold values from -6 to 6
- conductivity: float32 [1024, 1024], P('px', 'py'), may hold values from 0.2 to 1
Outputs:
- new_fields: bfloat16 [4, 16, 1024, 1024], P(None, None, 'px', 'py')
- new_solid: float32 [1024, 1024], P('px', 'py')
The draws below stay inside these ranges and needn't reach their ends.
Inputs may be any that keep to these rules, and one draw needn't show every extreme that they name: `wall_owner`: at most 4 of one device's wall slots name the same owner, and some owner receives exactly 4 of them. `wall_tile`: A y-line of the sending device's own block, numbered z times its x cells plus its local x.
All inputs are finite; a program needn't handle non-finite values.
Results may differ from the reference program's by a relative error of at most 0.0054.
Values may be sent and summed in bfloat16 or wider, within the bound.
A program may use at most 64 MiB of HBM per device.

```python
import math
import jax
import jax.numpy as jnp
import numpy as np
from jax import lax

FIELDS = 4
NX = 1024
NY = 1024
NZ = 16
SR = 64
WALL_DEV = 128
COND_STEPS = 8
CAP = 4
SOLID_ROWS = 1024
N_PX = 16
N_PY = 8
DEVICES = 128


def operator_stack(key, width):
    first, second = jax.random.split(key, 2)
    noise = jax.random.normal(first, (3, width, width), jnp.float32) * 0.6 / jnp.sqrt(width * 1.0)
    diagonal = jax.random.uniform(second, (3, width), jnp.float32, 0.6, 1.4)
    matrix = noise + jnp.eye(width, dtype=jnp.float32)[None, :, :] * diagonal[:, :, None]
    return matrix.astype(jnp.bfloat16)


def draw_x_operators(key, part):
    return operator_stack(jax.random.fold_in(key, 11), NX)


def draw_y_operators(key, part):
    return operator_stack(jax.random.fold_in(key, 23), NY)


def with_ends(drawn, rng, least, top_value):
    spot = [jax.random.randint(jax.random.fold_in(rng, axis), (), 0, length) for axis, length in enumerate(drawn.shape)]
    main_axis = drawn.shape.index(max(drawn.shape))
    beside = spot[:main_axis] + [(spot[main_axis] + 1) % drawn.shape[main_axis]] + spot[main_axis + 1:]
    return drawn.at[tuple(spot)].set(least).at[tuple(beside)].set(top_value)


def steps_of(own_key, dims, cuts, smallest, top_value):
    def one(axis_at, shards_of):
        heights = jax.random.uniform(jax.random.fold_in(jax.random.fold_in(own_key, 6), axis_at), (shards_of,), jnp.float32, smallest / len(cuts), top_value / len(cuts))
        return jnp.repeat(jnp.exp(heights), dims[axis_at] // shards_of).reshape((-1,) + (1,) * (len(dims) - axis_at - 1))

    factor_of = one(*cuts[0])
    for cut in cuts[1:]:
        factor_of = factor_of * one(*cut)
    return factor_of


def assign_block(key, own, number, rows, amount, top, most, skew):
    order = jax.random.permutation(key, amount)
    packed, common = load_shares(amount, rows * top, most, skew, True), load_shares(amount, rows * top, most, skew, False)
    places = jnp.arange(amount)

    def named(lengths, rotation):
        used = int((lengths > 0).sum())
        fixed = max(1, used // 4)
        passed = fixed + (places - fixed + rotation * (used - fixed)) % max(1, amount - fixed)
        return jnp.zeros((amount,), jnp.int32).at[order[jnp.where(places < fixed, places, passed)]].set(jnp.asarray(lengths, jnp.int32))

    lengths = jnp.where(number % 4 == 0, named(packed, number // 4), named(common, number - number // 4 - 1))
    mixed = jax.random.permutation(jax.random.fold_in(own, 3), amount)
    donor, sink = mixed[0:amount // 2 * 2:2], mixed[1:amount // 2 * 2:2]
    margin = jnp.minimum(lengths[donor] - 1, most - lengths[sink]) // 2
    margin = jnp.where((donor == order[0]) | (sink == order[0]) | (lengths[sink] == 0), 0, jnp.maximum(margin, 0))
    passed = jax.random.randint(jax.random.fold_in(own, 4), (amount // 2,), 0, 1 << 20) % (margin + 1)
    lengths = lengths.at[donor].add(-passed).at[sink].add(passed)
    labels = jnp.searchsorted(jnp.cumsum(lengths), jnp.arange(rows * top), side="right").astype(jnp.int32)
    table = labels.reshape(top, rows).T
    table = table[jax.random.permutation(jax.random.fold_in(own, 1), rows)]
    rotation = jax.random.randint(jax.random.fold_in(own, 2), (rows, 1), 0, top)
    return jnp.take_along_axis(table, (jnp.arange(top)[None, :] + rotation) % top, axis=1)


def load_shares(count, total, limit, slope, full):
    loads = [(1 << 20) // math.isqrt(standing ** slope) + 1 for standing in range(1, count + 1)]
    largest = limit if full else min(limit, max(-(-total // count), total * loads[0] // sum(loads)))
    least = 1 if total - largest >= count - 1 else 0
    counts, surplus = [largest] + [least] * (count - 1), total - largest - least * (count - 1)
    while surplus > 0:
        movable = [i for i in range(1, count) if counts[i] < largest] or [i for i in range(1, count) if counts[i] < limit]
        mass, remaining = sum([loads[i] for i in movable]), surplus
        for i in movable:
            addition = min(limit - counts[i], max(1, remaining * loads[i] // mass), surplus)
            counts[i] = counts[i] + addition
            surplus = surplus - addition
    return np.array(counts)


def gaussian(rng, shape, scale, reach, cuts=(), held_as=jnp.bfloat16):
    drawn = jax.random.normal(rng, shape, jnp.float32) * scale
    if len(cuts) > 0:
        drawn = steps_of(rng, shape, cuts, -0.22, 0.18) * drawn
    return jnp.clip(drawn, min=-reach, max=reach).astype(held_as)


def setup_inputs(seed: int = 0) -> dict:
    keys = jax.random.split(jax.random.key(seed), 10)
    fields = gaussian(keys[0], (FIELDS, NZ, NX, NY), 1.0, 6.0, ((2, 16), (3, 8)))
    x_operators = draw_x_operators(jax.random.fold_in(keys[9], 71), 0)
    y_operators = draw_y_operators(jax.random.fold_in(keys[9], 71), 0)
    viscosity = jnp.clip(jnp.exp(jax.random.uniform(keys[3], (FIELDS,), jnp.float32, math.log(0.1), math.log(1.0))), 0.1, 1.0)
    wall_tile = with_ends(jax.random.randint(keys[4], (DEVICES * WALL_DEV,), 0, NZ * (NX // N_PX)), jax.random.fold_in(keys[4], 1), 0, (NZ * (NX // N_PX)) - 1).astype(jnp.int32)
    wall_owner_keys = jax.random.split(jax.random.fold_in(keys[5], 1), (DEVICES * WALL_DEV) // WALL_DEV)
    wall_owner_turns = jax.random.permutation(jax.random.fold_in(keys[5], 3), (DEVICES * WALL_DEV) // WALL_DEV)
    wall_owner = jax.vmap(lambda own, number: assign_block(jax.random.fold_in(keys[5], 2), own, number, WALL_DEV, DEVICES, 1, CAP, 2))(wall_owner_keys, wall_owner_turns).reshape((DEVICES * WALL_DEV, 1))
    wall_row = with_ends(jax.random.randint(keys[6], (DEVICES * WALL_DEV,), 0, SR), jax.random.fold_in(keys[6], 1), 0, SR - 1).astype(jnp.int32)
    solid_temp = gaussian(keys[7], (SOLID_ROWS, NY), 1.0, 6.0, ((0, 16), (1, 8)), jnp.float32)
    conductivity = jnp.clip(jnp.exp(math.log(1.0) - 1.609438 * jax.random.uniform(keys[8], (SOLID_ROWS, NY), jnp.float32) ** steps_of(keys[8], (SOLID_ROWS, NY), ((0, 16), (1, 8)), -0.2, 0.2)), 0.2, 1.0)
    return dict(fields=fields, x_operators=x_operators, y_operators=y_operators, viscosity=viscosity, wall_tile=wall_tile, wall_owner=wall_owner, wall_row=wall_row, solid_temp=solid_temp, conductivity=conductivity)


time_step = 0.25
wall_gain = 0.5
diffusion_rate = 0.24
source_gain = 0.1


def pass_x(fields, operators, viscosity):
    mats = operators.astype(jnp.float32)
    speed = fields[0].astype(jnp.float32)

    def single(pair):
        field, rate = pair
        values = field.astype(jnp.float32)
        result = jnp.einsum('oij,zjy->oziy', mats, values, precision=lax.Precision.HIGHEST)
        return (result[2] + time_step * (-speed * result[0] + rate * result[1])).astype(jnp.bfloat16)

    return lax.map(single, (fields, viscosity))


def pass_y(fields, operators, viscosity):
    mats = operators.astype(jnp.float32)
    speed = fields[1].astype(jnp.float32)

    def single(pair):
        field, rate = pair
        values = field.astype(jnp.float32)
        result = jnp.einsum('oij,zxj->ozxi', mats, values, precision=lax.Precision.HIGHEST)
        return (result[2] + time_step * (-speed * result[0] + rate * result[1])).astype(jnp.bfloat16)

    return lax.map(single, (fields, viscosity))


def reference(fields, x_operators, y_operators, viscosity, wall_tile, wall_owner, wall_row, solid_temp, conductivity):
    half_step = pass_x(fields, x_operators, viscosity)
    new_fields = pass_y(half_step, y_operators, viscosity)
    cells_x = NX // N_PX
    cells_y = NY // N_PY
    sender = jnp.arange(DEVICES * WALL_DEV, dtype=jnp.int32) // WALL_DEV
    send_px = sender // N_PY
    send_py = sender % N_PY
    layer = wall_tile // cells_x
    column_x = send_px * cells_x + wall_tile % cells_x
    offsets = jnp.arange(cells_y, dtype=jnp.int32)
    theta = new_fields[3]
    values = theta[layer[:, None], column_x[:, None], send_py[:, None] * cells_y + offsets[None, :]]
    flux = wall_gain * values.astype(jnp.float32)
    owner = wall_owner[:, 0]
    target_row = (owner // N_PY) * SR + wall_row
    target_col = (owner % N_PY) * cells_y
    source = jnp.zeros(solid_temp.shape, jnp.float32)
    source = source.at[target_row[:, None], target_col[:, None] + offsets[None, :]].add(flux)
    temp = solid_temp
    kpad = jnp.pad(conductivity, 1)
    for _ in range(COND_STEPS):
        tpad = jnp.pad(temp, 1)
        near = [(tpad[2:, 1:-1], kpad[2:, 1:-1]), (tpad[:-2, 1:-1], kpad[:-2, 1:-1]),
                (tpad[1:-1, 2:], kpad[1:-1, 2:]), (tpad[1:-1, :-2], kpad[1:-1, :-2])]
        laplace = jnp.zeros(temp.shape, jnp.float32)
        for tnear, knear in near:
            laplace = laplace + 0.5 * (conductivity + knear) * (tnear - temp)
        temp = temp + diffusion_rate * laplace + source_gain * source
    return new_fields, temp
```

```python
import jax
import jax.numpy as jnp
from jax import lax
from jax.experimental import pallas as pl
from jax.experimental.pallas import tpu as pltpu
from jax.sharding import PartitionSpec as P

COND_STEPS = 8
time_step = 0.25
wall_gain = 0.5
diffusion_rate = 0.24
source_gain = 0.1

NPX = 16
NPY = 8
DEV = NPX * NPY
F = 4
NZ = 16
XB = 64
YB = 128
SLOT = 8
HALO = 8
ROWS = XB + 2 * HALO
COLS = 3 * YB
TILE = 256
MESH = pl.DeviceIdType.MESH
BF = jnp.bfloat16
F32 = jnp.float32


def iota(shape, axis):
    return lax.broadcasted_iota(jnp.int32, shape, axis)


def kernel(
    fields,
    xop_hbm,
    yop_hbm,
    visc,
    tile_ref,
    owner_ref,
    row_ref,
    temp_hbm,
    cond_hbm,
    out,
    solid_out,
    xop,
    yop,
    xrows,
    half,
    yrows,
    ysend,
    theta,
    gather,
    place,
    tags,
    wsend,
    wrecv,
    t_ext,
    k_ext,
    s_ext,
    load_sem,
    s1,
    r1,
    s2,
    r2,
    s4,
    r4,
    sw,
    rw,
    sh,
    rh,
    copy_sem,
    all_in,
):
    a = lax.axis_index("px")
    b = lax.axis_index("py")
    me = a * NPY + b
    held = a // 2
    par = a % 2
    is_self = held == b

    bar = pltpu.get_barrier_semaphore()

    @pl.loop(1, NPX)
    def _(d):
        pl.semaphore_signal(
            bar, inc=1, device_id=((a + d) % NPX, b), device_id_type=MESH
        )

    @pl.loop(1, NPY)
    def _(d):
        pl.semaphore_signal(
            bar, inc=1, device_id=(a, (b + d) % NPY), device_id_type=MESH
        )

    xload = pltpu.make_async_copy(xop_hbm, xop, load_sem.at[0])
    yload = pltpu.make_async_copy(yop_hbm, yop, load_sem.at[1])
    xload.start()
    yload.start()

    pl.semaphore_wait(bar, NPX + NPY - 2)

    def send_x(f):
        @pl.loop(1, NPX)
        def _(d):
            t = (a + d) % NPX
            pltpu.make_async_remote_copy(
                src_ref=fields.at[f, t],
                dst_ref=xrows.at[f, pl.ds(a * XB, XB)],
                send_sem=s1.at[f],
                recv_sem=r1.at[f],
                device_id=(t, b),
                device_id_type=MESH,
            ).start()

        pltpu.make_async_copy(
            fields.at[f, a], xrows.at[f, pl.ds(a * XB, XB)], r1.at[f]
        ).start()

    def wait_bytes(ref, sem):
        pltpu.make_async_copy(ref, ref, sem).wait()

    send_x(0)

    @pl.loop(1, NPX)
    def _(d):
        pl.semaphore_signal(
            all_in, inc=1, device_id=((a + d) % NPX, b), device_id_type=MESH
        )

    send_x(1)
    send_x(3)

    own = jnp.broadcast_to(owner_ref[...], (YB, YB))
    match = own == iota((YB, YB), 0)
    upper = (iota((YB, YB), 0) < iota((YB, YB), 1)).astype(F32).astype(BF)
    onehot = match.astype(F32)
    earlier = jnp.dot(onehot.astype(BF), upper, preferred_element_type=F32)
    pos = jnp.sum(earlier * onehot, axis=0, keepdims=True)
    dest = owner_ref[...].astype(F32) * SLOT + pos
    line = iota((DEV * SLOT, YB), 0).astype(F32)
    place[...] = (line == dest).astype(F32).astype(BF)
    tagged = jnp.where(line == dest + 4.0, row_ref[...].astype(F32) + 1.0, 0.0)
    tags[...] = jnp.dot(
        tagged.astype(BF), jnp.ones((YB, YB), BF), preferred_element_type=F32
    )
    tcol = jnp.broadcast_to(tile_ref[...].astype(F32), (YB, YB)).T
    for n in range(NZ * XB // YB):
        gather[:, n * YB : (n + 1) * YB] = (
            (tcol == (iota((YB, YB), 1) + n * YB).astype(F32)).astype(F32).astype(BF)
        )

    pl.semaphore_wait(all_in, NPX - 1)

    def around():
        for dr in (-1, 0, 1):
            for dc in (-1, 0, 1):
                if dr or dc:
                    yield dr, dc

    def halo(src, r0, dst, ssem, rsem):
        for dr, dc in around():
            if dr == 0:
                rows, to = pl.ds(r0, XB), pl.ds(HALO, XB)
            elif dr == 1:
                rows, to = pl.ds(r0 + XB - HALO, HALO), pl.ds(0, HALO)
            else:
                rows, to = pl.ds(r0, HALO), pl.ds(HALO + XB, HALO)
            cols = pl.ds((1 - dc) * YB, YB)
            view = src.at[rows] if r0 == 0 else src.at[rows, pl.ds(YB, YB)]
            pltpu.make_async_remote_copy(
                src_ref=view,
                dst_ref=dst.at[to, cols],
                send_sem=ssem,
                recv_sem=rsem,
                device_id=((a + dr + NPX) % NPX, (b + dc + NPY) % NPY),
                device_id_type=MESH,
            ).start()

    def halo_wait(dst, ssem, rsem, own_block):
        amount = 6 * HALO + 2 * XB
        flat = xrows.at[0, pl.ds(0, 2 * amount)]
        wait_bytes(flat, ssem)
        if own_block:
            amount += XB
        wait_bytes(xrows.at[0, pl.ds(0, 2 * amount)], rsem)

    centre = (pl.ds(HALO, XB), pl.ds(YB, YB))
    halo(temp_hbm, 0, t_ext, sh.at[0], rh.at[0])
    halo(cond_hbm, 0, k_ext, sh.at[1], rh.at[1])
    pltpu.make_async_copy(temp_hbm, t_ext.at[centre], rh.at[0]).start()
    pltpu.make_async_copy(cond_hbm, k_ext.at[centre], rh.at[1]).start()

    def send_half(f, tile):
        @pl.loop(0, TILE // XB)
        def _(j):
            t = tile * (TILE // XB) + j
            src = half.at[f, pl.ds(t * XB, XB)]
            dst = yrows.at[f, b, pl.ds(par * XB, XB)]
            local = jnp.logical_and(is_self, t == a)

            @pl.when(local)
            def _():
                pltpu.make_async_copy(src, dst, r2.at[f]).start()

            @pl.when(jnp.logical_not(local))
            def _():
                pltpu.make_async_remote_copy(
                    src_ref=src,
                    dst_ref=dst,
                    send_sem=s2.at[f],
                    recv_sem=r2.at[f],
                    device_id=(t, held),
                    device_id_type=MESH,
                ).start()

    def tile_x(f, tile):
        rr = pl.ds(pl.multiple_of(tile * TILE, TILE), TILE)
        q = xrows[f]
        r0 = jnp.dot(xop[0, rr, :], q, preferred_element_type=F32)
        r1_ = jnp.dot(xop[1, rr, :], q, preferred_element_type=F32)
        r2_ = jnp.dot(xop[2, rr, :], q, preferred_element_type=F32)
        speed = xrows[0, rr, :].astype(F32)
        half[f, rr, :] = (
            r2_ + time_step * (-speed * r0 + visc[f] * r1_)
        ).astype(BF)

    tiles = NPX * XB // TILE

    def pass_x(f):
        first = a // 4
        tile_x(f, first)

        @pl.loop(1, tiles)
        def _(i):
            tile_x(f, (first + i) % tiles)
            send_half(f, (first + i - 1) % tiles)

        send_half(f, (first + tiles - 1) % tiles)

    def send_y(f, tile):
        for j in range(TILE // YB):
            t = tile * (TILE // YB) + j
            src = ysend.at[f, t]
            if f == 3:
                dst = theta.at[pl.ds(2 * b, 2)]
            else:
                dst = out.at[f, pl.ds(2 * b, 2)]

            @pl.when(t == b)
            def _():
                pltpu.make_async_copy(src, dst, r4.at[f]).start()

            @pl.when(t != b)
            def _():
                pltpu.make_async_remote_copy(
                    src_ref=src,
                    dst_ref=dst,
                    send_sem=s4.at[f],
                    recv_sem=r4.at[f],
                    device_id=(a, t),
                    device_id_type=MESH,
                ).start()

    nt = (((1,), (1,)), ((), ()))

    def tile_y(f, tile):
        rr = pl.ds(pl.multiple_of(tile * TILE, TILE), TILE)
        q = jnp.concatenate([yrows[f, n] for n in range(NPY)], axis=1)
        r0 = lax.dot_general(q, yop[0, rr, :], nt, preferred_element_type=F32)
        r1_ = lax.dot_general(q, yop[1, rr, :], nt, preferred_element_type=F32)
        r2_ = lax.dot_general(q, yop[2, rr, :], nt, preferred_element_type=F32)
        for j in range(TILE // YB):
            t = tile * (TILE // YB) + j
            cc = slice(j * YB, (j + 1) * YB)
            speed = yrows[1, t].astype(F32)
            new = r2_[:, cc] + time_step * (
                -speed * r0[:, cc] + visc[f] * r1_[:, cc]
            )
            ysend[f, t] = new.astype(BF).reshape(2, XB, YB)

    ytiles = NPY * YB // TILE

    def pass_y(f):
        first = b // 2
        tile_y(f, first)

        @pl.loop(1, ytiles)
        def _(i):
            tile_y(f, (first + i) % ytiles)
            send_y(f, (first + i - 1) % ytiles)

        send_y(f, (first + ytiles - 1) % ytiles)

    def got_x(f):
        wait_bytes(xrows.at[f], r1.at[f])

    def got_half(f):
        wait_bytes(yrows.at[f], r2.at[f])

    xload.wait()
    got_x(0)
    got_x(1)
    pass_x(1)
    got_x(3)
    pass_x(3)
    send_x(2)
    pass_x(0)

    halo_wait(t_ext, sh.at[0], rh.at[0], True)
    halo_wait(k_ext, sh.at[1], rh.at[1], True)
    grow = iota((ROWS, COLS), 0) + (a * XB - HALO)
    gcol = iota((ROWS, COLS), 1) + (b * YB - YB)
    inside = (
        (grow >= 0) & (grow < NPX * XB) & (gcol >= 0) & (gcol < NPY * YB)
    )
    k_ext[...] = jnp.where(inside, k_ext[...], 0.0)
    t_ext[...] = jnp.where(inside, t_ext[...], 0.0)

    yload.wait()
    got_half(1)
    got_half(3)
    pass_y(3)
    pass_y(1)
    got_x(2)
    pass_x(2)
    got_half(0)
    pass_y(0)

    wait_bytes(theta, r4.at[3])
    keep_theta = pltpu.make_async_copy(theta, out.at[3], copy_sem)
    keep_theta.start()
    lines = theta[...].reshape(NZ * XB, YB)
    flux = jnp.dot(gather[...], lines, preferred_element_type=F32).astype(BF)
    wsend[...] = (
        jnp.dot(place[...], flux, preferred_element_type=F32) + tags[...]
    ).astype(BF)

    @pl.loop(1, DEV)
    def _(d):
        t = (me + d) % DEV
        pltpu.make_async_remote_copy(
            src_ref=wsend.at[pl.ds(t * SLOT, SLOT)],
            dst_ref=wrecv.at[pl.ds(me * SLOT, SLOT)],
            send_sem=sw,
            recv_sem=rw,
            device_id=(t // NPY, t % NPY),
            device_id_type=MESH,
        ).start()

    pltpu.make_async_copy(
        wsend.at[pl.ds(me * SLOT, SLOT)], wrecv.at[pl.ds(me * SLOT, SLOT)], rw
    ).start()

    got_half(2)
    pass_y(2)

    wait_bytes(wrecv, rw)
    arrived = wrecv[...]
    named = pltpu.roll(arrived.astype(F32), DEV * SLOT - 4, 0)
    mine = iota((DEV * SLOT, YB), 0) % SLOT < 4
    select = jnp.where(
        mine & (named == (iota((DEV * SLOT, YB), 1) + 1).astype(F32)), 1.0, 0.0
    ).astype(BF)
    source = lax.dot_general(
        select, arrived, (((0,), (0,)), ((), ())), preferred_element_type=F32
    )[:XB]
    s_ext[HALO : HALO + XB, YB : 2 * YB] = source * (source_gain * wall_gain)

    kappa = k_ext[...]

    def north(v):
        return pltpu.roll(v, 1, 0)

    def south(v):
        return pltpu.roll(v, ROWS - 1, 0)

    def west(v):
        return pltpu.roll(v, 1, 1)

    def east(v):
        return pltpu.roll(v, COLS - 1, 1)

    rate = 0.5 * diffusion_rate
    sides = (north, south, west, east)
    coef = [
        jnp.where(inside, rate * (kappa + side(kappa)), 0.0) for side in sides
    ]
    stay = 1.0 - (coef[0] + coef[1] + coef[2] + coef[3])

    halo(s_ext, HALO, s_ext, sh.at[2], rh.at[2])
    halo_wait(s_ext, sh.at[2], rh.at[2], False)

    heat = jnp.where(inside, s_ext[...], 0.0)
    temp = t_ext[...]
    for _ in range(COND_STEPS):
        new = stay * temp + heat
        for c, side in zip(coef, sides):
            new = new + c * side(temp)
        temp = new
    solid_out[...] = temp[HALO : HALO + XB, YB : 2 * YB]

    for f in range(3):
        wait_bytes(out.at[f], r4.at[f])
    keep_theta.wait()
    for f in range(F):
        wait_bytes(xrows.at[f, pl.ds(0, XB * (NPX - 1))], s1.at[f])

        @pl.when(is_self)
        def _():
            wait_bytes(half.at[f, pl.ds(0, XB * (NPX - 1))], s2.at[f])

        @pl.when(jnp.logical_not(is_self))
        def _():
            wait_bytes(half.at[f], s2.at[f])

        wait_bytes(ysend.at[f, pl.ds(0, NPY - 1)], s4.at[f])
    wait_bytes(wsend.at[pl.ds(0, (DEV - 1) * SLOT)], sw)


def on_device(
    fields,
    x_operators,
    y_operators,
    viscosity,
    wall_tile,
    wall_owner,
    wall_row,
    solid_temp,
    conductivity,
):
    any_ = pl.BlockSpec(memory_space=pl.ANY)
    vmem = pl.BlockSpec(memory_space=pltpu.VMEM)
    smem = pl.BlockSpec(memory_space=pltpu.SMEM)
    dma = pltpu.SemaphoreType.DMA
    new_fields, new_solid = pl.pallas_call(
        kernel,
        out_shape=(
            jax.ShapeDtypeStruct(fields.shape, BF),
            jax.ShapeDtypeStruct(solid_temp.shape, F32),
        ),
        in_specs=[any_, any_, any_, smem, vmem, vmem, vmem, any_, any_],
        out_specs=(any_, vmem),
        scratch_shapes=[
            pltpu.VMEM((3, NPX * XB, NPX * XB), BF),
            pltpu.VMEM((3, NPY * YB, NPY * YB), BF),
            pltpu.VMEM((F, NPX * XB, YB), BF),
            pltpu.VMEM((F, NPX * XB, YB), BF),
            pltpu.VMEM((F, NPY, 2 * XB, YB), BF),
            pltpu.VMEM((F, NPY, 2, XB, YB), BF),
            pltpu.VMEM((NZ, XB, YB), BF),
            pltpu.VMEM((YB, NZ * XB), BF),
            pltpu.VMEM((DEV * SLOT, YB), BF),
            pltpu.VMEM((DEV * SLOT, YB), F32),
            pltpu.VMEM((DEV * SLOT, YB), BF),
            pltpu.VMEM((DEV * SLOT, YB), BF),
            pltpu.VMEM((ROWS, COLS), F32),
            pltpu.VMEM((ROWS, COLS), F32),
            pltpu.VMEM((ROWS, COLS), F32),
            dma((2,)),
            dma((F,)),
            dma((F,)),
            dma((F,)),
            dma((F,)),
            dma((F,)),
            dma((F,)),
            dma,
            dma,
            dma((3,)),
            dma((3,)),
            dma,
            pltpu.SemaphoreType.REGULAR,
        ],
        compiler_params=pltpu.CompilerParams(
            collective_id=0, has_side_effects=True, vmem_limit_bytes=48 << 20
        ),
        name="substep",
    )(
        fields,
        x_operators,
        y_operators,
        viscosity,
        wall_tile.reshape(1, -1),
        wall_owner.reshape(1, -1),
        wall_row.reshape(1, -1),
        solid_temp,
        conductivity,
    )
    return new_fields, new_solid


def solution(mesh):
    return jax.shard_map(
        on_device,
        mesh=mesh,
        in_specs=(
            P(None, None, "px", "py"),
            P(),
            P(),
            P(),
            P(("px", "py")),
            P(("px", "py"), None),
            P(("px", "py")),
            P("px", "py"),
            P("px", "py"),
        ),
        out_specs=(P(None, None, "px", "py"), P("px", "py")),
        check_vma=False,
    )
```

```python
import jax
import jax.numpy as jnp
from jax import lax
from jax.experimental import pallas as pl
from jax.experimental.pallas import tpu as pltpu
from jax.sharding import PartitionSpec as P

COND_STEPS = 8
time_step = 0.25
wall_gain = 0.5
diffusion_rate = 0.24
source_gain = 0.1

NPX = 16
NPY = 8
DEV = NPX * NPY
F = 4
NZ = 16
XB = 64
YB = 128
CAP = 4
LINES = NPX * CAP
SLOTS = DEV * CAP
HALO = 8
ROWS = XB + 2 * HALO
COLS = 3 * YB
TILE = 256
MESH = pl.DeviceIdType.MESH
BF = jnp.bfloat16
F32 = jnp.float32


def iota(shape, axis):
    return lax.broadcasted_iota(jnp.int32, shape, axis)


def kernel(
    fields,
    xop_hbm,
    yop_hbm,
    visc_hbm,
    tile_hbm,
    owner_hbm,
    row_hbm,
    temp_hbm,
    cond_hbm,
    out,
    solid_out,
    visc,
    tile_ref,
    owner_ref,
    row_ref,
    solid,
    xop,
    yop,
    yopt,
    xrows,
    half,
    yrows,
    ysend,
    theta,
    gather,
    place,
    perm,
    select,
    tsend,
    tmid,
    tturn,
    ttag,
    wsend,
    wmid,
    wturn,
    wrecv,
    t_ext,
    k_ext,
    s_ext,
    coef,
    load_sem,
    s1,
    r1,
    s2,
    r2,
    s4,
    r4,
    sw,
    rw,
    sh,
    rh,
    copy_sem,
    all_in,
):
    a = lax.axis_index("px")
    b = lax.axis_index("py")
    me = a * NPY + b
    held = a // 2
    par = a % 2
    is_self = held == b

    bar = pltpu.get_barrier_semaphore()

    @pl.loop(1, NPX)
    def _(d):
        pl.semaphore_signal(
            bar, inc=1, device_id=((a + d) % NPX, b), device_id_type=MESH
        )

    @pl.loop(1, NPY)
    def _(d):
        pl.semaphore_signal(
            bar, inc=1, device_id=(a, (b + d) % NPY), device_id_type=MESH
        )

    xload = pltpu.make_async_copy(xop_hbm, xop, load_sem.at[0])
    yload = pltpu.make_async_copy(yop_hbm, yop, load_sem.at[1])
    small = [
        pltpu.make_async_copy(src, dst, load_sem.at[2 + n])
        for n, (src, dst) in enumerate(
            (
                (visc_hbm, visc),
                (tile_hbm, tile_ref),
                (owner_hbm, owner_ref),
                (row_hbm, row_ref),
            )
        )
    ]
    for load in small:
        load.start()
    xload.start()
    yload.start()

    pl.semaphore_wait(bar, NPX + NPY - 2)

    def send_x(f):
        @pl.loop(1, NPX)
        def _(d):
            t = (a + d) % NPX
            pltpu.make_async_remote_copy(
                src_ref=fields.at[f, t],
                dst_ref=xrows.at[f, pl.ds(a * XB, XB)],
                send_sem=s1.at[f],
                recv_sem=r1.at[f],
                device_id=(t, b),
                device_id_type=MESH,
            ).start()

        pltpu.make_async_copy(
            fields.at[f, a], xrows.at[f, pl.ds(a * XB, XB)], r1.at[f]
        ).start()

    def wait_bytes(ref, sem):
        pltpu.make_async_copy(ref, ref, sem).wait()

    send_x(0)

    @pl.loop(1, NPX)
    def _(d):
        pl.semaphore_signal(
            all_in, inc=1, device_id=((a + d) % NPX, b), device_id_type=MESH
        )

    send_x(1)
    send_x(3)

    for load in small:
        load.wait()
    own = jnp.broadcast_to(owner_ref[...], (YB, YB))
    match = own == iota((YB, YB), 0)
    upper = (iota((YB, YB), 0) < iota((YB, YB), 1)).astype(F32).astype(BF)
    onehot = match.astype(F32)
    earlier = jnp.dot(onehot.astype(BF), upper, preferred_element_type=F32)
    pos = jnp.sum(earlier * onehot, axis=0, keepdims=True)
    owner = owner_ref[...]
    to_a = (owner // NPY).astype(F32) * CAP + pos
    to_b = (owner % NPY).astype(F32)
    dest = to_b * LINES + to_a
    place[...] = (iota((SLOTS, YB), 0).astype(F32) == dest).astype(F32).astype(BF)
    name = row_ref[...].astype(F32) + 1.0
    named = jnp.where(
        (iota((NPY * 8, YB), 0) // 8).astype(F32) == to_b, name, 0.0
    ).astype(BF)
    spot = (iota((YB, YB), 0).astype(F32) == to_a).astype(F32).astype(BF)
    tsend[...] = lax.dot_general(
        named, spot, (((1,), (1,)), ((), ())), preferred_element_type=F32
    ).astype(BF)

    def along_y(src, dst, size, n):
        @pl.loop(1, NPY)
        def _(d):
            t = (b + d) % NPY
            pltpu.make_async_remote_copy(
                src_ref=src.at[pl.ds(t * size, size)],
                dst_ref=dst.at[pl.ds(b * size, size)],
                send_sem=sw.at[n],
                recv_sem=rw.at[n],
                device_id=(a, t),
                device_id_type=MESH,
            ).start()

        pltpu.make_async_copy(
            src.at[pl.ds(b * size, size)], dst.at[pl.ds(b * size, size)], rw.at[n]
        ).start()

    def along_x(src, dst, size, n):
        @pl.loop(1, NPX)
        def _(d):
            t = (a + d) % NPX
            pltpu.make_async_remote_copy(
                src_ref=src.at[pl.ds(t * size, size)],
                dst_ref=dst.at[pl.ds(a * size, size)],
                send_sem=sw.at[n],
                recv_sem=rw.at[n],
                device_id=(t, b),
                device_id_type=MESH,
            ).start()

        pltpu.make_async_copy(
            src.at[pl.ds(a * size, size)], dst.at[pl.ds(a * size, size)], rw.at[n]
        ).start()

    along_y(tsend, tmid, 8, 2)
    r_to = iota((SLOTS, SLOTS), 0)
    perm[...] = (
        (
            iota((SLOTS, SLOTS), 1)
            == ((r_to % (NPY * CAP)) // CAP) * LINES
            + (r_to // (NPY * CAP)) * CAP
            + r_to % CAP
        )
        .astype(F32)
        .astype(BF)
    )
    tcol = jnp.broadcast_to(tile_ref[...].astype(F32), (YB, YB)).T
    for n in range(NZ * XB // YB):
        gather[:, n * YB : (n + 1) * YB] = (
            (tcol == (iota((YB, YB), 1) + n * YB).astype(F32)).astype(F32).astype(BF)
        )

    pl.semaphore_wait(all_in, NPX - 1)

    def around():
        for dr in (-1, 0, 1):
            for dc in (-1, 0, 1):
                if dr or dc:
                    yield dr, dc

    def halo(src, r0, dst, ssem, rsem):
        for dr, dc in around():
            if dr == 0:
                rows, to = pl.ds(r0, XB), pl.ds(HALO, XB)
            elif dr == 1:
                rows, to = pl.ds(r0 + XB - HALO, HALO), pl.ds(0, HALO)
            else:
                rows, to = pl.ds(r0, HALO), pl.ds(HALO + XB, HALO)
            cols = pl.ds((1 - dc) * YB, YB)
            view = src.at[rows] if r0 == 0 else src.at[rows, pl.ds(YB, YB)]
            pltpu.make_async_remote_copy(
                src_ref=view,
                dst_ref=dst.at[to, cols],
                send_sem=ssem,
                recv_sem=rsem,
                device_id=((a + dr + NPX) % NPX, (b + dc + NPY) % NPY),
                device_id_type=MESH,
            ).start()

    def halo_wait(dst, ssem, rsem, own_block):
        amount = 6 * HALO + 2 * XB
        flat = xrows.at[0, pl.ds(0, 2 * amount)]
        wait_bytes(flat, ssem)
        if own_block:
            amount += XB
        wait_bytes(xrows.at[0, pl.ds(0, 2 * amount)], rsem)

    centre = (pl.ds(HALO, XB), pl.ds(YB, YB))
    halo(temp_hbm, 0, t_ext, sh.at[0], rh.at[0])
    halo(cond_hbm, 0, k_ext, sh.at[1], rh.at[1])
    pltpu.make_async_copy(temp_hbm, t_ext.at[centre], rh.at[0]).start()
    pltpu.make_async_copy(cond_hbm, k_ext.at[centre], rh.at[1]).start()

    def send_half(f, tile):
        @pl.loop(0, TILE // XB)
        def _(j):
            t = tile * (TILE // XB) + j
            src = half.at[f, pl.ds(t * XB, XB)]
            dst = yrows.at[f, b, pl.ds(par * XB, XB)]
            local = jnp.logical_and(is_self, t == a)

            @pl.when(local)
            def _():
                pltpu.make_async_copy(src, dst, r2.at[f]).start()

            @pl.when(jnp.logical_not(local))
            def _():
                pltpu.make_async_remote_copy(
                    src_ref=src,
                    dst_ref=dst,
                    send_sem=s2.at[f],
                    recv_sem=r2.at[f],
                    device_id=(t, held),
                    device_id_type=MESH,
                ).start()

    def tile_x(f, tile):
        rr = pl.ds(pl.multiple_of(tile * TILE, TILE), TILE)
        q = xrows[f]
        r0 = jnp.dot(xop[0, rr, :], q, preferred_element_type=F32)
        r1_ = jnp.dot(xop[1, rr, :], q, preferred_element_type=F32)
        r2_ = jnp.dot(xop[2, rr, :], q, preferred_element_type=F32)
        speed = xrows[0, rr, :].astype(F32)
        half[f, rr, :] = (
            r2_ + time_step * (-speed * r0 + visc[f] * r1_)
        ).astype(BF)

    tiles = NPX * XB // TILE

    def far_first(i):
        return (2 - i) * (1 - i // 2) + 3 * (3 - i) * (i // 2)


    def pass_x(f):
        def turn(i):
            return (a // 4 + far_first(i)) % tiles

        tile_x(f, turn(0))

        @pl.loop(1, tiles)
        def _(i):
            tile_x(f, turn(i))
            send_half(f, turn(i - 1))

        send_half(f, turn(tiles - 1))

    def send_y(f, tile):
        for j in range(TILE // YB):
            t = tile * (TILE // YB) + j
            src = ysend.at[f, t]
            if f == 3:
                dst = theta.at[pl.ds(2 * b, 2)]
            else:
                dst = out.at[f, pl.ds(2 * b, 2)]

            @pl.when(t == b)
            def _():
                pltpu.make_async_copy(src, dst, r4.at[f]).start()

            @pl.when(t != b)
            def _():
                pltpu.make_async_remote_copy(
                    src_ref=src,
                    dst_ref=dst,
                    send_sem=s4.at[f],
                    recv_sem=r4.at[f],
                    device_id=(a, t),
                    device_id_type=MESH,
                ).start()

    def tile_y(f, tile):
        rr = pl.ds(pl.multiple_of(tile * TILE, TILE), TILE)
        q = jnp.concatenate([yrows[f, n] for n in range(NPY)], axis=1)
        r0 = jnp.dot(q, yopt[0, :, rr], preferred_element_type=F32)
        r1_ = jnp.dot(q, yopt[1, :, rr], preferred_element_type=F32)
        r2_ = jnp.dot(q, yopt[2, :, rr], preferred_element_type=F32)
        for j in range(TILE // YB):
            t = tile * (TILE // YB) + j
            cc = slice(j * YB, (j + 1) * YB)
            speed = yrows[1, t].astype(F32)
            new = r2_[:, cc] + time_step * (
                -speed * r0[:, cc] + visc[f] * r1_[:, cc]
            )
            ysend[f, t] = new.astype(BF).reshape(2, XB, YB)

    ytiles = NPY * YB // TILE

    def pass_y(f):
        def turn(i):
            return (b // 2 + far_first(i)) % ytiles

        tile_y(f, turn(0))

        @pl.loop(1, ytiles)
        def _(i):
            tile_y(f, turn(i))
            send_y(f, turn(i - 1))

        send_y(f, turn(ytiles - 1))

    def got_x(f):
        wait_bytes(xrows.at[f], r1.at[f])

    def got_half(f):
        wait_bytes(yrows.at[f], r2.at[f])

    yload.wait()

    @pl.loop(0, NPY * YB // TILE)
    def _(n):
        rr = pl.ds(pl.multiple_of(n * TILE, TILE), TILE)
        for k in range(3):
            for j in range(NPY * YB // TILE):
                cc = slice(j * TILE, (j + 1) * TILE)
                yopt[k, cc, rr] = yop[k, rr, cc].T

    wait_bytes(tmid, rw.at[2])
    lane = iota((NPY * 8, YB), 1)
    from_b = iota((NPY * 8, YB), 0)
    pick = (from_b == ((lane % 32) // CAP) * 8) & (lane // 32 == a % 4)
    cross = lax.dot_general(
        tmid[...],
        pick.astype(F32).astype(BF),
        (((0,), (0,)), ((), ())),
        preferred_element_type=F32,
    )
    same = iota((YB, YB), 0) % CAP == iota((YB, YB), 1) % CAP
    group = iota((YB, YB), 0) // 8 == iota((YB, YB), 1) // CAP
    tturn[...] = jnp.dot(
        group.astype(F32).astype(BF),
        jnp.where(same, cross, 0.0).astype(BF),
        preferred_element_type=F32,
    ).astype(BF)
    along_x(tturn, ttag, 8, 3)

    xload.wait()
    got_x(0)
    got_x(1)
    pass_x(1)
    got_x(3)
    pass_x(3)
    pass_x(0)
    send_x(2)

    wait_bytes(ttag, rw.at[3])
    for n in range(SLOTS // YB):
        tag = jnp.zeros((8, YB), F32)
        for k in range(4):
            tag = tag + ttag[(4 * n + k) * 8 : (4 * n + k + 1) * 8, :].astype(F32)
        select[:, n * YB : (n + 1) * YB] = (
            (jnp.broadcast_to(tag[:1], (XB, YB)) == (iota((XB, YB), 0) + 1).astype(F32))
            .astype(F32)
            .astype(BF)
        )

    halo_wait(t_ext, sh.at[0], rh.at[0], True)
    halo_wait(k_ext, sh.at[1], rh.at[1], True)
    grow = iota((ROWS, COLS), 0) + (a * XB - HALO)
    gcol = iota((ROWS, COLS), 1) + (b * YB - YB)
    inside = (
        (grow >= 0) & (grow < NPX * XB) & (gcol >= 0) & (gcol < NPY * YB)
    )
    kappa = jnp.where(inside, k_ext[...], 0.0)
    t_ext[...] = jnp.where(inside, t_ext[...], 0.0)

    def north(v):
        return pltpu.roll(v, 1, 0)

    def south(v):
        return pltpu.roll(v, ROWS - 1, 0)

    def west(v):
        return pltpu.roll(v, 1, 1)

    def east(v):
        return pltpu.roll(v, COLS - 1, 1)

    rate = 0.5 * diffusion_rate
    sides = (north, south, west, east)
    total = jnp.zeros((ROWS, COLS), F32)
    for n, side in enumerate(sides):
        part = jnp.where(inside, rate * (kappa + side(kappa)), 0.0)
        coef[1 + n] = part
        total = total + part
    coef[0] = 1.0 - total


    got_half(1)
    got_half(3)
    pass_y(3)
    pass_y(1)

    wait_bytes(theta, r4.at[3])
    keep_theta = pltpu.make_async_copy(theta, out.at[3], copy_sem)
    keep_theta.start()
    lines = theta[...].reshape(NZ * XB, YB)
    flux = jnp.dot(gather[...], lines, preferred_element_type=F32).astype(BF)
    wsend[...] = jnp.dot(place[...], flux, preferred_element_type=F32).astype(BF)
    along_y(wsend, wmid, LINES, 0)

    got_x(2)
    pass_x(2)
    wait_bytes(wmid, rw.at[0])
    wturn[...] = jnp.dot(perm[...], wmid[...], preferred_element_type=F32).astype(BF)
    along_x(wturn, wrecv, NPY * CAP, 1)

    got_half(0)
    pass_y(0)
    got_half(2)
    pass_y(2)

    wait_bytes(wrecv, rw.at[1])
    source = jnp.dot(select[...], wrecv[...], preferred_element_type=F32)
    s_ext[HALO : HALO + XB, YB : 2 * YB] = source * (source_gain * wall_gain)

    halo(s_ext, HALO, s_ext, sh.at[2], rh.at[2])
    halo_wait(s_ext, sh.at[2], rh.at[2], False)

    heat = jnp.where(inside, s_ext[...], 0.0)
    temp = t_ext[...]
    for _ in range(COND_STEPS):
        new = coef[0] * temp + heat
        for n, side in enumerate(sides):
            new = new + coef[1 + n] * side(temp)
        temp = new
    solid[...] = temp[HALO : HALO + XB, YB : 2 * YB]
    keep_solid = pltpu.make_async_copy(solid, solid_out, load_sem.at[0])
    keep_solid.start()

    for f in range(3):
        wait_bytes(out.at[f], r4.at[f])
    keep_theta.wait()
    keep_solid.wait()
    for f in range(F):
        wait_bytes(xrows.at[f, pl.ds(0, XB * (NPX - 1))], s1.at[f])

        @pl.when(is_self)
        def _():
            wait_bytes(half.at[f, pl.ds(0, XB * (NPX - 1))], s2.at[f])

        @pl.when(jnp.logical_not(is_self))
        def _():
            wait_bytes(half.at[f], s2.at[f])

        wait_bytes(ysend.at[f, pl.ds(0, NPY - 1)], s4.at[f])
    wait_bytes(wsend.at[pl.ds(0, (NPY - 1) * LINES)], sw.at[0])
    wait_bytes(wturn.at[pl.ds(0, (NPX - 1) * NPY * CAP)], sw.at[1])
    wait_bytes(tsend.at[pl.ds(0, (NPY - 1) * 8)], sw.at[2])
    wait_bytes(tturn.at[pl.ds(0, (NPX - 1) * 8)], sw.at[3])


def finish(fields_in, solid_in, fields_out, solid_out, held, solid, sem_in, sem_out):
    pieces = [
        (fields_in.at[f], held.at[f], fields_out.at[f]) for f in range(F)
    ] + [(solid_in, solid, solid_out)]
    loads = [
        pltpu.make_async_copy(src, mid, sem_in.at[n])
        for n, (src, mid, _) in enumerate(pieces)
    ]
    stores = [
        pltpu.make_async_copy(mid, dst, sem_out.at[n])
        for n, (_, mid, dst) in enumerate(pieces)
    ]
    for load in loads:
        load.start()
    for load, store in zip(loads, stores):
        load.wait()
        store.start()
    for store in stores:
        store.wait()


def on_device(
    fields,
    x_operators,
    y_operators,
    viscosity,
    wall_tile,
    wall_owner,
    wall_row,
    solid_temp,
    conductivity,
):
    hbm = pl.BlockSpec(memory_space=pltpu.HBM)
    dma = pltpu.SemaphoreType.DMA
    new_fields, new_solid = pl.pallas_call(
        kernel,
        out_shape=(
            jax.ShapeDtypeStruct(fields.shape, BF),
            jax.ShapeDtypeStruct(solid_temp.shape, F32),
        ),
        in_specs=[hbm] * 9,
        out_specs=(hbm, hbm),
        scratch_shapes=[
            pltpu.SMEM((F,), F32),
            pltpu.VMEM((1, YB), jnp.int32),
            pltpu.VMEM((1, YB), jnp.int32),
            pltpu.VMEM((1, YB), jnp.int32),
            pltpu.VMEM((XB, YB), F32),
            pltpu.VMEM((3, NPX * XB, NPX * XB), BF),
            pltpu.VMEM((3, NPY * YB, NPY * YB), BF),
            pltpu.VMEM((3, NPY * YB, NPY * YB), BF),
            pltpu.VMEM((F, NPX * XB, YB), BF),
            pltpu.VMEM((F, NPX * XB, YB), BF),
            pltpu.VMEM((F, NPY, 2 * XB, YB), BF),
            pltpu.VMEM((F, NPY, 2, XB, YB), BF),
            pltpu.VMEM((NZ, XB, YB), BF),
            pltpu.VMEM((YB, NZ * XB), BF),
            pltpu.VMEM((SLOTS, YB), BF),
            pltpu.VMEM((SLOTS, SLOTS), BF),
            pltpu.VMEM((XB, SLOTS), BF),
            pltpu.VMEM((NPY * 8, YB), BF),
            pltpu.VMEM((NPY * 8, YB), BF),
            pltpu.VMEM((NPX * 8, YB), BF),
            pltpu.VMEM((NPX * 8, YB), BF),
            pltpu.VMEM((SLOTS, YB), BF),
            pltpu.VMEM((SLOTS, YB), BF),
            pltpu.VMEM((SLOTS, YB), BF),
            pltpu.VMEM((SLOTS, YB), BF),
            pltpu.VMEM((ROWS, COLS), F32),
            pltpu.VMEM((ROWS, COLS), F32),
            pltpu.VMEM((ROWS, COLS), F32),
            pltpu.VMEM((5, ROWS, COLS), F32),
            dma((6,)),
            dma((F,)),
            dma((F,)),
            dma((F,)),
            dma((F,)),
            dma((F,)),
            dma((F,)),
            dma((4,)),
            dma((4,)),
            dma((3,)),
            dma((3,)),
            dma,
            pltpu.SemaphoreType.REGULAR,
        ],
        compiler_params=pltpu.CompilerParams(
            collective_id=0, has_side_effects=True, vmem_limit_bytes=67_043_328
        ),
        name="substep",
    )(
        fields,
        x_operators,
        y_operators,
        viscosity,
        wall_tile.reshape(1, -1),
        wall_owner.reshape(1, -1),
        wall_row.reshape(1, -1),
        solid_temp,
        conductivity,
    )
    return pl.pallas_call(
        finish,
        out_shape=(
            jax.ShapeDtypeStruct(fields.shape, BF),
            jax.ShapeDtypeStruct(solid_temp.shape, F32),
        ),
        in_specs=[hbm] * 2,
        out_specs=(hbm, hbm),
        scratch_shapes=[
            pltpu.VMEM((F, NZ, XB, YB), BF),
            pltpu.VMEM((XB, YB), F32),
            dma((F + 1,)),
            dma((F + 1,)),
        ],
        compiler_params=pltpu.CompilerParams(vmem_limit_bytes=67_043_328),
        name="finish",
    )(new_fields, new_solid)


def solution(mesh):
    return jax.shard_map(
        on_device,
        mesh=mesh,
        in_specs=(
            P(None, None, "px", "py"),
            P(),
            P(),
            P(),
            P(("px", "py")),
            P(("px", "py"), None),
            P(("px", "py")),
            P("px", "py"),
            P("px", "py"),
        ),
        out_specs=(P(None, None, "px", "py"), P("px", "py")),
        check_vma=False,
    )
```

```python
import jax
import jax.numpy as jnp
from jax import lax
from jax.experimental import pallas as pl
from jax.experimental.pallas import tpu as pltpu
from jax.sharding import PartitionSpec as P

COND_STEPS = 8
time_step = 0.25
wall_gain = 0.5
diffusion_rate = 0.24
source_gain = 0.1

NPX = 16
NPY = 8
DEV = NPX * NPY
F = 4
NZ = 16
XB = 64
YB = 128
CAP = 4
LINES = NPX * CAP
SLOTS = DEV * CAP
HALO = 8
ROWS = XB + 2 * HALO
COLS = 3 * YB
TILE = 256
MESH = pl.DeviceIdType.MESH
BF = jnp.bfloat16
F32 = jnp.float32


def iota(shape, axis):
    return lax.broadcasted_iota(jnp.int32, shape, axis)


def kernel(
    fields,
    xop_hbm,
    yop_hbm,
    visc_hbm,
    tile_hbm,
    owner_hbm,
    row_hbm,
    temp_hbm,
    cond_hbm,
    out,
    solid_out,
    visc,
    tile_ref,
    owner_ref,
    row_ref,
    solid,
    xop,
    yop,
    yopt,
    xrows,
    half,
    yrows,
    ysend,
    theta,
    gather,
    place,
    select,
    tsend,
    tmid,
    tturn,
    ttag,
    wsend,
    wrecv,
    t_ext,
    k_ext,
    s_ext,
    coef,
    load_sem,
    s1,
    r1,
    s2,
    r2,
    s4,
    r4,
    sw,
    rw,
    sh,
    rh,
    copy_sem,
    all_in,
):
    a = lax.axis_index("px")
    b = lax.axis_index("py")
    me = a * NPY + b
    held = a // 2
    par = a % 2
    is_self = held == b

    bar = pltpu.get_barrier_semaphore()

    @pl.loop(1, NPX)
    def _(d):
        pl.semaphore_signal(
            bar, inc=1, device_id=((a + d) % NPX, b), device_id_type=MESH
        )

    @pl.loop(1, NPY)
    def _(d):
        pl.semaphore_signal(
            bar, inc=1, device_id=(a, (b + d) % NPY), device_id_type=MESH
        )

    xload = pltpu.make_async_copy(xop_hbm, xop, load_sem.at[0])
    yload = pltpu.make_async_copy(yop_hbm, yop, load_sem.at[1])
    small = [
        pltpu.make_async_copy(src, dst, load_sem.at[2 + n])
        for n, (src, dst) in enumerate(
            (
                (visc_hbm, visc),
                (tile_hbm, tile_ref),
                (owner_hbm, owner_ref),
                (row_hbm, row_ref),
            )
        )
    ]
    for load in small:
        load.start()
    xload.start()
    yload.start()

    pl.semaphore_wait(bar, NPX + NPY - 2)

    def send_x(f):
        @pl.loop(1, NPX)
        def _(d):
            t = (a + d) % NPX
            pltpu.make_async_remote_copy(
                src_ref=fields.at[f, t],
                dst_ref=xrows.at[f, pl.ds(a * XB, XB)],
                send_sem=s1.at[f],
                recv_sem=r1.at[f],
                device_id=(t, b),
                device_id_type=MESH,
            ).start()

        pltpu.make_async_copy(
            fields.at[f, a], xrows.at[f, pl.ds(a * XB, XB)], r1.at[f]
        ).start()

    def wait_bytes(ref, sem):
        pltpu.make_async_copy(ref, ref, sem).wait()

    send_x(0)

    @pl.loop(1, NPX)
    def _(d):
        pl.semaphore_signal(
            all_in, inc=1, device_id=((a + d) % NPX, b), device_id_type=MESH
        )

    send_x(1)
    send_x(3)

    for load in small:
        load.wait()
    own = jnp.broadcast_to(owner_ref[...], (YB, YB))
    match = own == iota((YB, YB), 0)
    upper = (iota((YB, YB), 0) < iota((YB, YB), 1)).astype(F32).astype(BF)
    onehot = match.astype(F32)
    earlier = jnp.dot(onehot.astype(BF), upper, preferred_element_type=F32)
    pos = jnp.sum(earlier * onehot, axis=0, keepdims=True)
    owner = owner_ref[...]
    to_a = (owner // NPY).astype(F32) * CAP + pos
    to_b = (owner % NPY).astype(F32)
    dest = owner.astype(F32) * CAP + pos
    place[...] = (iota((SLOTS, YB), 0).astype(F32) == dest).astype(F32).astype(BF)
    name = row_ref[...].astype(F32) + 1.0
    named = jnp.where(
        (iota((NPY * 8, YB), 0) // 8).astype(F32) == to_b, name, 0.0
    ).astype(BF)
    spot = (iota((YB, YB), 0).astype(F32) == to_a).astype(F32).astype(BF)
    tsend[...] = lax.dot_general(
        named, spot, (((1,), (1,)), ((), ())), preferred_element_type=F32
    ).astype(BF)

    def along_y(src, dst, size, n):
        @pl.loop(1, NPY)
        def _(d):
            t = (b + d) % NPY
            pltpu.make_async_remote_copy(
                src_ref=src.at[pl.ds(t * size, size)],
                dst_ref=dst.at[pl.ds(b * size, size)],
                send_sem=sw.at[n],
                recv_sem=rw.at[n],
                device_id=(a, t),
                device_id_type=MESH,
            ).start()

        pltpu.make_async_copy(
            src.at[pl.ds(b * size, size)], dst.at[pl.ds(b * size, size)], rw.at[n]
        ).start()

    def along_x(src, dst, size, n):
        @pl.loop(1, NPX)
        def _(d):
            t = (a + d) % NPX
            pltpu.make_async_remote_copy(
                src_ref=src.at[pl.ds(t * size, size)],
                dst_ref=dst.at[pl.ds(a * size, size)],
                send_sem=sw.at[n],
                recv_sem=rw.at[n],
                device_id=(t, b),
                device_id_type=MESH,
            ).start()

        pltpu.make_async_copy(
            src.at[pl.ds(a * size, size)], dst.at[pl.ds(a * size, size)], rw.at[n]
        ).start()

    along_y(tsend, tmid, 8, 2)
    tcol = jnp.broadcast_to(tile_ref[...].astype(F32), (YB, YB)).T
    for n in range(NZ * XB // YB):
        gather[:, n * YB : (n + 1) * YB] = (
            (tcol == (iota((YB, YB), 1) + n * YB).astype(F32)).astype(F32).astype(BF)
        )

    pl.semaphore_wait(all_in, NPX - 1)

    def around():
        for dr in (-1, 0, 1):
            for dc in (-1, 0, 1):
                if dr or dc:
                    yield dr, dc

    def halo(src, r0, dst, ssem, rsem):
        for dr, dc in around():
            if dr == 0:
                rows, to = pl.ds(r0, XB), pl.ds(HALO, XB)
            elif dr == 1:
                rows, to = pl.ds(r0 + XB - HALO, HALO), pl.ds(0, HALO)
            else:
                rows, to = pl.ds(r0, HALO), pl.ds(HALO + XB, HALO)
            cols = pl.ds((1 - dc) * YB, YB)
            view = src.at[rows] if r0 == 0 else src.at[rows, pl.ds(YB, YB)]
            pltpu.make_async_remote_copy(
                src_ref=view,
                dst_ref=dst.at[to, cols],
                send_sem=ssem,
                recv_sem=rsem,
                device_id=((a + dr + NPX) % NPX, (b + dc + NPY) % NPY),
                device_id_type=MESH,
            ).start()

    def halo_wait(dst, ssem, rsem, own_block):
        amount = 6 * HALO + 2 * XB
        flat = xrows.at[0, pl.ds(0, 2 * amount)]
        wait_bytes(flat, ssem)
        if own_block:
            amount += XB
        wait_bytes(xrows.at[0, pl.ds(0, 2 * amount)], rsem)

    centre = (pl.ds(HALO, XB), pl.ds(YB, YB))
    halo(temp_hbm, 0, t_ext, sh.at[0], rh.at[0])
    halo(cond_hbm, 0, k_ext, sh.at[1], rh.at[1])
    pltpu.make_async_copy(temp_hbm, t_ext.at[centre], rh.at[0]).start()
    pltpu.make_async_copy(cond_hbm, k_ext.at[centre], rh.at[1]).start()

    def send_half(f, tile):
        @pl.loop(0, TILE // XB)
        def _(j):
            t = tile * (TILE // XB) + j
            src = half.at[f, pl.ds(t * XB, XB)]
            dst = yrows.at[f, b, pl.ds(par * XB, XB)]
            local = jnp.logical_and(is_self, t == a)

            @pl.when(local)
            def _():
                pltpu.make_async_copy(src, dst, r2.at[f]).start()

            @pl.when(jnp.logical_not(local))
            def _():
                pltpu.make_async_remote_copy(
                    src_ref=src,
                    dst_ref=dst,
                    send_sem=s2.at[f],
                    recv_sem=r2.at[f],
                    device_id=(t, held),
                    device_id_type=MESH,
                ).start()

    def tile_x(f, tile):
        rr = pl.ds(pl.multiple_of(tile * TILE, TILE), TILE)
        q = xrows[f]
        r0 = jnp.dot(xop[0, rr, :], q, preferred_element_type=F32)
        r1_ = jnp.dot(xop[1, rr, :], q, preferred_element_type=F32)
        r2_ = jnp.dot(xop[2, rr, :], q, preferred_element_type=F32)
        speed = xrows[0, rr, :].astype(F32)
        half[f, rr, :] = (
            r2_ + time_step * (-speed * r0 + visc[f] * r1_)
        ).astype(BF)

    tiles = NPX * XB // TILE

    def far_first(i):
        return (2 - i) * (1 - i // 2) + 3 * (3 - i) * (i // 2)


    def pass_x(f):
        def turn(i):
            return (a // 4 + far_first(i)) % tiles

        tile_x(f, turn(0))

        @pl.loop(1, tiles)
        def _(i):
            tile_x(f, turn(i))
            send_half(f, turn(i - 1))

        send_half(f, turn(tiles - 1))

    def send_y(f, tile):
        for j in range(TILE // YB):
            t = tile * (TILE // YB) + j
            src = ysend.at[f, t]
            if f == 3:
                dst = theta.at[pl.ds(2 * b, 2)]
            else:
                dst = out.at[f, pl.ds(2 * b, 2)]

            @pl.when(t == b)
            def _():
                pltpu.make_async_copy(src, dst, r4.at[f]).start()

            @pl.when(t != b)
            def _():
                pltpu.make_async_remote_copy(
                    src_ref=src,
                    dst_ref=dst,
                    send_sem=s4.at[f],
                    recv_sem=r4.at[f],
                    device_id=(a, t),
                    device_id_type=MESH,
                ).start()

    def tile_y(f, tile):
        rr = pl.ds(pl.multiple_of(tile * TILE, TILE), TILE)
        q = jnp.concatenate([yrows[f, n] for n in range(NPY)], axis=1)
        r0 = jnp.dot(q, yopt[0, :, rr], preferred_element_type=F32)
        r1_ = jnp.dot(q, yopt[1, :, rr], preferred_element_type=F32)
        r2_ = jnp.dot(q, yopt[2, :, rr], preferred_element_type=F32)
        for j in range(TILE // YB):
            t = tile * (TILE // YB) + j
            cc = slice(j * YB, (j + 1) * YB)
            speed = yrows[1, t].astype(F32)
            new = r2_[:, cc] + time_step * (
                -speed * r0[:, cc] + visc[f] * r1_[:, cc]
            )
            ysend[f, t] = new.astype(BF).reshape(2, XB, YB)

    ytiles = NPY * YB // TILE

    def pass_y(f):
        def turn(i):
            return (b // 2 + far_first(i)) % ytiles

        tile_y(f, turn(0))

        @pl.loop(1, ytiles)
        def _(i):
            tile_y(f, turn(i))
            send_y(f, turn(i - 1))

        send_y(f, turn(ytiles - 1))

    def got_x(f):
        wait_bytes(xrows.at[f], r1.at[f])

    def got_half(f):
        wait_bytes(yrows.at[f], r2.at[f])

    yload.wait()

    @pl.loop(0, NPY * YB // TILE)
    def _(n):
        rr = pl.ds(pl.multiple_of(n * TILE, TILE), TILE)
        for k in range(3):
            for j in range(NPY * YB // TILE):
                cc = slice(j * TILE, (j + 1) * TILE)
                yopt[k, cc, rr] = yop[k, rr, cc].T

    wait_bytes(tmid, rw.at[2])
    lane = iota((NPY * 8, YB), 1)
    from_b = iota((NPY * 8, YB), 0)
    pick = (from_b == ((lane % 32) // CAP) * 8) & (lane // 32 == a % 4)
    cross = lax.dot_general(
        tmid[...],
        pick.astype(F32).astype(BF),
        (((0,), (0,)), ((), ())),
        preferred_element_type=F32,
    )
    same = iota((YB, YB), 0) % CAP == iota((YB, YB), 1) % CAP
    group = iota((YB, YB), 0) // 8 == iota((YB, YB), 1) // CAP
    tturn[...] = jnp.dot(
        group.astype(F32).astype(BF),
        jnp.where(same, cross, 0.0).astype(BF),
        preferred_element_type=F32,
    ).astype(BF)
    along_x(tturn, ttag, 8, 3)

    xload.wait()
    got_x(0)
    got_x(1)
    pass_x(1)
    got_x(3)
    pass_x(3)
    pass_x(0)
    send_x(2)

    wait_bytes(ttag, rw.at[3])
    for n in range(SLOTS // YB):
        tag = jnp.zeros((8, YB), F32)
        for k in range(4):
            tag = tag + ttag[(4 * n + k) * 8 : (4 * n + k + 1) * 8, :].astype(F32)
        select[:, n * YB : (n + 1) * YB] = (
            (jnp.broadcast_to(tag[:1], (XB, YB)) == (iota((XB, YB), 0) + 1).astype(F32))
            .astype(F32)
            .astype(BF)
        )

    halo_wait(t_ext, sh.at[0], rh.at[0], True)
    halo_wait(k_ext, sh.at[1], rh.at[1], True)
    grow = iota((ROWS, COLS), 0) + (a * XB - HALO)
    gcol = iota((ROWS, COLS), 1) + (b * YB - YB)
    inside = (
        (grow >= 0) & (grow < NPX * XB) & (gcol >= 0) & (gcol < NPY * YB)
    )
    kappa = jnp.where(inside, k_ext[...], 0.0)
    t_ext[...] = jnp.where(inside, t_ext[...], 0.0)

    def north(v):
        return pltpu.roll(v, 1, 0)

    def south(v):
        return pltpu.roll(v, ROWS - 1, 0)

    def west(v):
        return pltpu.roll(v, 1, 1)

    def east(v):
        return pltpu.roll(v, COLS - 1, 1)

    rate = 0.5 * diffusion_rate
    sides = (north, south, west, east)
    total = jnp.zeros((ROWS, COLS), F32)
    for n, side in enumerate(sides):
        part = jnp.where(inside, rate * (kappa + side(kappa)), 0.0)
        coef[1 + n] = part
        total = total + part
    coef[0] = 1.0 - total


    got_half(1)
    got_half(3)
    pass_y(3)
    pass_y(1)
    got_x(2)
    pass_x(2)
    wait_bytes(theta, r4.at[3])
    keep_theta = pltpu.make_async_copy(theta, out.at[3], copy_sem)
    keep_theta.start()
    lines = theta[...].reshape(NZ * XB, YB)
    flux = jnp.dot(gather[...], lines, preferred_element_type=F32).astype(BF)
    wsend[...] = (
        jnp.dot(place[...], flux, preferred_element_type=F32)
        .reshape(DEV, CAP, YB)
        .astype(BF)
    )

    def send_wall(to_a, to_b):
        pltpu.make_async_remote_copy(
            src_ref=wsend.at[to_a * NPY + to_b],
            dst_ref=wrecv.at[me],
            send_sem=sw.at[0],
            recv_sem=rw.at[0],
            device_id=(to_a, to_b),
            device_id_type=MESH,
        ).start()

    near = [(b + n) % NPY for n in range(NPY)]

    @pl.loop(1, NPX)
    def _(d):
        for to_b in near:
            send_wall((a + d) % NPX, to_b)

    for to_b in near[1:]:
        send_wall(a, to_b)
    pltpu.make_async_copy(wsend.at[me], wrecv.at[me], rw.at[0]).start()

    got_half(0)
    pass_y(0)
    wait_bytes(wrecv, rw.at[0])
    arrived = wrecv[...].astype(F32).reshape(SLOTS, YB).astype(BF)
    source = jnp.dot(select[...], arrived, preferred_element_type=F32)
    s_ext[HALO : HALO + XB, YB : 2 * YB] = source * (source_gain * wall_gain)

    halo(s_ext, HALO, s_ext, sh.at[2], rh.at[2])
    got_half(2)
    pass_y(2)
    halo_wait(s_ext, sh.at[2], rh.at[2], False)

    heat = jnp.where(inside, s_ext[...], 0.0)
    temp = t_ext[...]
    for _ in range(COND_STEPS):
        new = coef[0] * temp + heat
        for n, side in enumerate(sides):
            new = new + coef[1 + n] * side(temp)
        temp = new
    solid[...] = temp[HALO : HALO + XB, YB : 2 * YB]
    keep_solid = pltpu.make_async_copy(solid, solid_out, load_sem.at[0])
    keep_solid.start()

    for f in range(3):
        wait_bytes(out.at[f], r4.at[f])
    keep_theta.wait()
    keep_solid.wait()
    for f in range(F):
        wait_bytes(xrows.at[f, pl.ds(0, XB * (NPX - 1))], s1.at[f])

        @pl.when(is_self)
        def _():
            wait_bytes(half.at[f, pl.ds(0, XB * (NPX - 1))], s2.at[f])

        @pl.when(jnp.logical_not(is_self))
        def _():
            wait_bytes(half.at[f], s2.at[f])

        wait_bytes(ysend.at[f, pl.ds(0, NPY - 1)], s4.at[f])
    wait_bytes(wsend.at[pl.ds(0, DEV - 1)], sw.at[0])
    wait_bytes(tsend.at[pl.ds(0, (NPY - 1) * 8)], sw.at[2])
    wait_bytes(tturn.at[pl.ds(0, (NPX - 1) * 8)], sw.at[3])


def finish(fields_in, solid_in, fields_out, solid_out, held, solid, sem_in, sem_out):
    pieces = [
        (fields_in.at[f], held.at[f], fields_out.at[f]) for f in range(F)
    ] + [(solid_in, solid, solid_out)]
    loads = [
        pltpu.make_async_copy(src, mid, sem_in.at[n])
        for n, (src, mid, _) in enumerate(pieces)
    ]
    stores = [
        pltpu.make_async_copy(mid, dst, sem_out.at[n])
        for n, (_, mid, dst) in enumerate(pieces)
    ]
    for load in loads:
        load.start()
    for load, store in zip(loads, stores):
        load.wait()
        store.start()
    for store in stores:
        store.wait()


def on_device(
    fields,
    x_operators,
    y_operators,
    viscosity,
    wall_tile,
    wall_owner,
    wall_row,
    solid_temp,
    conductivity,
):
    hbm = pl.BlockSpec(memory_space=pltpu.HBM)
    dma = pltpu.SemaphoreType.DMA
    new_fields, new_solid = pl.pallas_call(
        kernel,
        out_shape=(
            jax.ShapeDtypeStruct(fields.shape, BF),
            jax.ShapeDtypeStruct(solid_temp.shape, F32),
        ),
        in_specs=[hbm] * 9,
        out_specs=(hbm, hbm),
        scratch_shapes=[
            pltpu.SMEM((F,), F32),
            pltpu.VMEM((1, YB), jnp.int32),
            pltpu.VMEM((1, YB), jnp.int32),
            pltpu.VMEM((1, YB), jnp.int32),
            pltpu.VMEM((XB, YB), F32),
            pltpu.VMEM((3, NPX * XB, NPX * XB), BF),
            pltpu.VMEM((3, NPY * YB, NPY * YB), BF),
            pltpu.VMEM((3, NPY * YB, NPY * YB), BF),
            pltpu.VMEM((F, NPX * XB, YB), BF),
            pltpu.VMEM((F, NPX * XB, YB), BF),
            pltpu.VMEM((F, NPY, 2 * XB, YB), BF),
            pltpu.VMEM((F, NPY, 2, XB, YB), BF),
            pltpu.VMEM((NZ, XB, YB), BF),
            pltpu.VMEM((YB, NZ * XB), BF),
            pltpu.VMEM((SLOTS, YB), BF),
            pltpu.VMEM((XB, SLOTS), BF),
            pltpu.VMEM((NPY * 8, YB), BF),
            pltpu.VMEM((NPY * 8, YB), BF),
            pltpu.VMEM((NPX * 8, YB), BF),
            pltpu.VMEM((NPX * 8, YB), BF),
            pltpu.VMEM((DEV, CAP, YB), BF),
            pltpu.VMEM((DEV, CAP, YB), BF),
            pltpu.VMEM((ROWS, COLS), F32),
            pltpu.VMEM((ROWS, COLS), F32),
            pltpu.VMEM((ROWS, COLS), F32),
            pltpu.VMEM((5, ROWS, COLS), F32),
            dma((6,)),
            dma((F,)),
            dma((F,)),
            dma((F,)),
            dma((F,)),
            dma((F,)),
            dma((F,)),
            dma((4,)),
            dma((4,)),
            dma((3,)),
            dma((3,)),
            dma,
            pltpu.SemaphoreType.REGULAR,
        ],
        compiler_params=pltpu.CompilerParams(
            collective_id=0, has_side_effects=True, vmem_limit_bytes=67_043_328
        ),
        name="substep",
    )(
        fields,
        x_operators,
        y_operators,
        viscosity,
        wall_tile.reshape(1, -1),
        wall_owner.reshape(1, -1),
        wall_row.reshape(1, -1),
        solid_temp,
        conductivity,
    )
    return pl.pallas_call(
        finish,
        out_shape=(
            jax.ShapeDtypeStruct(fields.shape, BF),
            jax.ShapeDtypeStruct(solid_temp.shape, F32),
        ),
        in_specs=[hbm] * 2,
        out_specs=(hbm, hbm),
        scratch_shapes=[
            pltpu.VMEM((F, NZ, XB, YB), BF),
            pltpu.VMEM((XB, YB), F32),
            dma((F + 1,)),
            dma((F + 1,)),
        ],
        compiler_params=pltpu.CompilerParams(vmem_limit_bytes=67_043_328),
        name="finish",
    )(new_fields, new_solid)


def solution(mesh):
    return jax.shard_map(
        on_device,
        mesh=mesh,
        in_specs=(
            P(None, None, "px", "py"),
            P(),
            P(),
            P(),
            P(("px", "py")),
            P(("px", "py"), None),
            P(("px", "py")),
            P("px", "py"),
            P("px", "py"),
        ),
        out_specs=(P(None, None, "px", "py"), P("px", "py")),
        check_vma=False,
    )
```

```python
import jax
import jax.numpy as jnp
from jax import lax
from jax.experimental import pallas as pl
from jax.experimental.pallas import tpu as pltpu
from jax.sharding import PartitionSpec as P

COND_STEPS = 8
time_step = 0.25
wall_gain = 0.5
diffusion_rate = 0.24
source_gain = 0.1

NPX = 16
NPY = 8
DEV = NPX * NPY
F = 4
NZ = 16
XB = 64
YB = 128
CAP = 4
LINES = NPX * CAP
SLOTS = DEV * CAP
HALO = 8
ROWS = XB + 2 * HALO
COLS = 3 * YB
TILE = 256
MESH = pl.DeviceIdType.MESH
BF = jnp.bfloat16
F32 = jnp.float32


def iota(shape, axis):
    return lax.broadcasted_iota(jnp.int32, shape, axis)


def kernel(
    fields,
    xop_hbm,
    yop_hbm,
    visc_hbm,
    tile_hbm,
    owner_hbm,
    row_hbm,
    temp_hbm,
    cond_hbm,
    out,
    solid_out,
    visc,
    tile_ref,
    owner_ref,
    row_ref,
    solid,
    xop,
    yop,
    yopt,
    xsum,
    ysum,
    xrows,
    half,
    yrows,
    ysend,
    theta,
    gather,
    place,
    select,
    tsend,
    tmid,
    tturn,
    ttag,
    wsend,
    wrecv,
    t_ext,
    k_ext,
    s_ext,
    coef,
    load_sem,
    s1,
    r1,
    s2,
    r2,
    s4,
    r4,
    sw,
    rw,
    sh,
    rh,
    copy_sem,
    all_in,
):
    a = lax.axis_index("px")
    b = lax.axis_index("py")
    me = a * NPY + b
    held = a // 2
    par = a % 2
    is_self = held == b

    bar = pltpu.get_barrier_semaphore()

    @pl.loop(1, NPX)
    def _(d):
        pl.semaphore_signal(
            bar, inc=1, device_id=((a + d) % NPX, b), device_id_type=MESH
        )

    @pl.loop(1, NPY)
    def _(d):
        pl.semaphore_signal(
            bar, inc=1, device_id=(a, (b + d) % NPY), device_id_type=MESH
        )

    xload = pltpu.make_async_copy(xop_hbm, xop, load_sem.at[0])
    yload = pltpu.make_async_copy(yop_hbm, yop, load_sem.at[1])
    small = [
        pltpu.make_async_copy(src, dst, load_sem.at[2 + n])
        for n, (src, dst) in enumerate(
            (
                (visc_hbm, visc),
                (tile_hbm, tile_ref),
                (owner_hbm, owner_ref),
                (row_hbm, row_ref),
            )
        )
    ]
    for load in small:
        load.start()
    xload.start()
    yload.start()

    pl.semaphore_wait(bar, NPX + NPY - 2)

    def send_x(f):
        @pl.loop(1, NPX)
        def _(d):
            t = (a + d) % NPX
            pltpu.make_async_remote_copy(
                src_ref=fields.at[f, t],
                dst_ref=xrows.at[f, pl.ds(a * XB, XB)],
                send_sem=s1.at[f],
                recv_sem=r1.at[f],
                device_id=(t, b),
                device_id_type=MESH,
            ).start()

        pltpu.make_async_copy(
            fields.at[f, a], xrows.at[f, pl.ds(a * XB, XB)], r1.at[f]
        ).start()

    def wait_bytes(ref, sem):
        pltpu.make_async_copy(ref, ref, sem).wait()

    send_x(0)

    @pl.loop(1, NPX)
    def _(d):
        pl.semaphore_signal(
            all_in, inc=1, device_id=((a + d) % NPX, b), device_id_type=MESH
        )

    send_x(1)
    send_x(3)

    for load in small:
        load.wait()
    own = jnp.broadcast_to(owner_ref[...], (YB, YB))
    match = own == iota((YB, YB), 0)
    upper = (iota((YB, YB), 0) < iota((YB, YB), 1)).astype(F32).astype(BF)
    onehot = match.astype(F32)
    earlier = jnp.dot(onehot.astype(BF), upper, preferred_element_type=F32)
    pos = jnp.sum(earlier * onehot, axis=0, keepdims=True)
    owner = owner_ref[...]
    to_a = (owner // NPY).astype(F32) * CAP + pos
    to_b = (owner % NPY).astype(F32)
    dest = owner.astype(F32) * CAP + pos
    place[...] = (iota((SLOTS, YB), 0).astype(F32) == dest).astype(F32).astype(BF)
    name = row_ref[...].astype(F32) + 1.0
    named = jnp.where(
        (iota((NPY * 8, YB), 0) // 8).astype(F32) == to_b, name, 0.0
    ).astype(BF)
    spot = (iota((YB, YB), 0).astype(F32) == to_a).astype(F32).astype(BF)
    tsend[...] = lax.dot_general(
        named, spot, (((1,), (1,)), ((), ())), preferred_element_type=F32
    ).astype(BF)

    def along_y(src, dst, size, n):
        @pl.loop(1, NPY)
        def _(d):
            t = (b + d) % NPY
            pltpu.make_async_remote_copy(
                src_ref=src.at[pl.ds(t * size, size)],
                dst_ref=dst.at[pl.ds(b * size, size)],
                send_sem=sw.at[n],
                recv_sem=rw.at[n],
                device_id=(a, t),
                device_id_type=MESH,
            ).start()

        pltpu.make_async_copy(
            src.at[pl.ds(b * size, size)], dst.at[pl.ds(b * size, size)], rw.at[n]
        ).start()

    def along_x(src, dst, size, n):
        @pl.loop(1, NPX)
        def _(d):
            t = (a + d) % NPX
            pltpu.make_async_remote_copy(
                src_ref=src.at[pl.ds(t * size, size)],
                dst_ref=dst.at[pl.ds(a * size, size)],
                send_sem=sw.at[n],
                recv_sem=rw.at[n],
                device_id=(t, b),
                device_id_type=MESH,
            ).start()

        pltpu.make_async_copy(
            src.at[pl.ds(a * size, size)], dst.at[pl.ds(a * size, size)], rw.at[n]
        ).start()

    along_y(tsend, tmid, 8, 2)
    tcol = jnp.broadcast_to(tile_ref[...].astype(F32), (YB, YB)).T
    for n in range(NZ * XB // YB):
        gather[:, n * YB : (n + 1) * YB] = (
            (tcol == (iota((YB, YB), 1) + n * YB).astype(F32)).astype(F32).astype(BF)
        )

    pl.semaphore_wait(all_in, NPX - 1)

    def around():
        for dr in (-1, 0, 1):
            for dc in (-1, 0, 1):
                if dr or dc:
                    yield dr, dc

    def halo(src, r0, dst, ssem, rsem):
        for dr, dc in around():
            if dr == 0:
                rows, to = pl.ds(r0, XB), pl.ds(HALO, XB)
            elif dr == 1:
                rows, to = pl.ds(r0 + XB - HALO, HALO), pl.ds(0, HALO)
            else:
                rows, to = pl.ds(r0, HALO), pl.ds(HALO + XB, HALO)
            cols = pl.ds((1 - dc) * YB, YB)
            view = src.at[rows] if r0 == 0 else src.at[rows, pl.ds(YB, YB)]
            pltpu.make_async_remote_copy(
                src_ref=view,
                dst_ref=dst.at[to, cols],
                send_sem=ssem,
                recv_sem=rsem,
                device_id=((a + dr + NPX) % NPX, (b + dc + NPY) % NPY),
                device_id_type=MESH,
            ).start()

    def halo_wait(dst, ssem, rsem, own_block):
        amount = 6 * HALO + 2 * XB
        flat = xrows.at[0, pl.ds(0, 2 * amount)]
        wait_bytes(flat, ssem)
        if own_block:
            amount += XB
        wait_bytes(xrows.at[0, pl.ds(0, 2 * amount)], rsem)

    centre = (pl.ds(HALO, XB), pl.ds(YB, YB))
    halo(temp_hbm, 0, t_ext, sh.at[0], rh.at[0])
    halo(cond_hbm, 0, k_ext, sh.at[1], rh.at[1])
    pltpu.make_async_copy(temp_hbm, t_ext.at[centre], rh.at[0]).start()
    pltpu.make_async_copy(cond_hbm, k_ext.at[centre], rh.at[1]).start()

    def send_half(f, tile):
        @pl.loop(0, TILE // XB)
        def _(j):
            t = tile * (TILE // XB) + j
            src = half.at[f, pl.ds(t * XB, XB)]
            dst = yrows.at[f, b, pl.ds(par * XB, XB)]
            local = jnp.logical_and(is_self, t == a)

            @pl.when(local)
            def _():
                pltpu.make_async_copy(src, dst, r2.at[f]).start()

            @pl.when(jnp.logical_not(local))
            def _():
                pltpu.make_async_remote_copy(
                    src_ref=src,
                    dst_ref=dst,
                    send_sem=s2.at[f],
                    recv_sem=r2.at[f],
                    device_id=(t, held),
                    device_id_type=MESH,
                ).start()

    def tile_x(f, tile):
        rr = pl.ds(pl.multiple_of(tile * TILE, TILE), TILE)
        q = xrows[f]
        r0 = jnp.dot(xop[0, rr, :], q, preferred_element_type=F32)
        speed = xrows[0, rr, :].astype(F32)
        if f in (1, 3):
            rest = jnp.dot(xsum[f // 2, rr, :], q, preferred_element_type=F32)
            half[f, rr, :] = (rest - time_step * (speed * r0)).astype(BF)
        else:
            r1_ = jnp.dot(xop[1, rr, :], q, preferred_element_type=F32)
            r2_ = jnp.dot(xop[2, rr, :], q, preferred_element_type=F32)
            half[f, rr, :] = (
                r2_ + time_step * (-speed * r0 + visc[f] * r1_)
            ).astype(BF)

    tiles = NPX * XB // TILE

    def far_first(i):
        return (2 - i) * (1 - i // 2) + 3 * (3 - i) * (i // 2)


    def pass_x(f):
        def turn(i):
            return (a // 4 + far_first(i)) % tiles

        tile_x(f, turn(0))

        @pl.loop(1, tiles)
        def _(i):
            tile_x(f, turn(i))
            send_half(f, turn(i - 1))

        send_half(f, turn(tiles - 1))

    def send_y(f, tile):
        for j in range(TILE // YB):
            t = tile * (TILE // YB) + j
            src = ysend.at[f, t]
            if f == 3:
                dst = theta.at[pl.ds(2 * b, 2)]
            else:
                dst = out.at[f, pl.ds(2 * b, 2)]

            @pl.when(t == b)
            def _():
                pltpu.make_async_copy(src, dst, r4.at[f]).start()

            @pl.when(t != b)
            def _():
                pltpu.make_async_remote_copy(
                    src_ref=src,
                    dst_ref=dst,
                    send_sem=s4.at[f],
                    recv_sem=r4.at[f],
                    device_id=(a, t),
                    device_id_type=MESH,
                ).start()

    def tile_y(f, tile):
        rr = pl.ds(pl.multiple_of(tile * TILE, TILE), TILE)
        q = jnp.concatenate([yrows[f, n] for n in range(NPY)], axis=1)
        r0 = jnp.dot(q, yopt[0, :, rr], preferred_element_type=F32)
        r1_ = jnp.dot(q, yopt[1, :, rr], preferred_element_type=F32)
        r2_ = jnp.dot(q, yopt[2, :, rr], preferred_element_type=F32)
        for j in range(TILE // YB):
            t = tile * (TILE // YB) + j
            cc = slice(j * YB, (j + 1) * YB)
            speed = yrows[1, t].astype(F32)
            new = r2_[:, cc] + time_step * (
                -speed * r0[:, cc] + visc[f] * r1_[:, cc]
            )
            ysend[f, t] = new.astype(BF).reshape(2, XB, YB)

    ytiles = NPY * YB // TILE

    def pass_y(f):
        def turn(i):
            return (b // 2 + far_first(i)) % ytiles

        tile_y(f, turn(0))

        @pl.loop(1, ytiles)
        def _(i):
            tile_y(f, turn(i))
            send_y(f, turn(i - 1))

        send_y(f, turn(ytiles - 1))

    def got_x(f):
        wait_bytes(xrows.at[f], r1.at[f])

    def got_half(f):
        wait_bytes(yrows.at[f], r2.at[f])

    yload.wait()

    @pl.loop(0, NPY * YB // TILE)
    def _(n):
        rr = pl.ds(pl.multiple_of(n * TILE, TILE), TILE)
        for k in range(3):
            for j in range(NPY * YB // TILE):
                cc = slice(j * TILE, (j + 1) * TILE)
                yopt[k, cc, rr] = yop[k, rr, cc].T

    wait_bytes(tmid, rw.at[2])
    lane = iota((NPY * 8, YB), 1)
    from_b = iota((NPY * 8, YB), 0)
    pick = (from_b == ((lane % 32) // CAP) * 8) & (lane // 32 == a % 4)
    cross = lax.dot_general(
        tmid[...],
        pick.astype(F32).astype(BF),
        (((0,), (0,)), ((), ())),
        preferred_element_type=F32,
    )
    same = iota((YB, YB), 0) % CAP == iota((YB, YB), 1) % CAP
    group = iota((YB, YB), 0) // 8 == iota((YB, YB), 1) // CAP
    tturn[...] = jnp.dot(
        group.astype(F32).astype(BF),
        jnp.where(same, cross, 0.0).astype(BF),
        preferred_element_type=F32,
    ).astype(BF)
    along_x(tturn, ttag, 8, 3)

    xload.wait()

    @pl.loop(0, NPX * XB // 32)
    def _(n):
        rr = pl.ds(pl.multiple_of(n * 32, 32), 32)
        second = time_step * xop[1, rr, :].astype(F32)
        smooth = xop[2, rr, :].astype(F32)
        xsum[0, rr, :] = (smooth + visc[1] * second).astype(BF)
        xsum[1, rr, :] = (smooth + visc[3] * second).astype(BF)

    got_x(0)
    got_x(1)
    pass_x(1)
    got_x(3)
    pass_x(3)
    pass_x(0)
    send_x(2)

    wait_bytes(ttag, rw.at[3])
    for n in range(SLOTS // YB):
        tag = jnp.zeros((8, YB), F32)
        for k in range(4):
            tag = tag + ttag[(4 * n + k) * 8 : (4 * n + k + 1) * 8, :].astype(F32)
        select[:, n * YB : (n + 1) * YB] = (
            (jnp.broadcast_to(tag[:1], (XB, YB)) == (iota((XB, YB), 0) + 1).astype(F32))
            .astype(F32)
            .astype(BF)
        )

    halo_wait(t_ext, sh.at[0], rh.at[0], True)
    halo_wait(k_ext, sh.at[1], rh.at[1], True)
    grow = iota((ROWS, COLS), 0) + (a * XB - HALO)
    gcol = iota((ROWS, COLS), 1) + (b * YB - YB)
    inside = (
        (grow >= 0) & (grow < NPX * XB) & (gcol >= 0) & (gcol < NPY * YB)
    )
    kappa = jnp.where(inside, k_ext[...], 0.0)
    t_ext[...] = jnp.where(inside, t_ext[...], 0.0)

    def north(v):
        return pltpu.roll(v, 1, 0)

    def south(v):
        return pltpu.roll(v, ROWS - 1, 0)

    def west(v):
        return pltpu.roll(v, 1, 1)

    def east(v):
        return pltpu.roll(v, COLS - 1, 1)

    rate = 0.5 * diffusion_rate
    sides = (north, south, west, east)
    total = jnp.zeros((ROWS, COLS), F32)
    for n, side in enumerate(sides):
        part = jnp.where(inside, rate * (kappa + side(kappa)), 0.0)
        coef[1 + n] = part
        total = total + part
    coef[0] = 1.0 - total


    got_half(1)
    got_half(3)
    pass_y(3)
    pass_y(1)
    got_x(2)
    pass_x(2)
    wait_bytes(theta, r4.at[3])
    keep_theta = pltpu.make_async_copy(theta, out.at[3], copy_sem)
    keep_theta.start()
    lines = theta[...].reshape(NZ * XB, YB)
    flux = jnp.dot(gather[...], lines, preferred_element_type=F32).astype(BF)
    wsend[...] = (
        jnp.dot(place[...], flux, preferred_element_type=F32)
        .reshape(DEV, CAP, YB)
        .astype(BF)
    )

    def send_wall(to_a, to_b):
        pltpu.make_async_remote_copy(
            src_ref=wsend.at[to_a * NPY + to_b],
            dst_ref=wrecv.at[me],
            send_sem=sw.at[0],
            recv_sem=rw.at[0],
            device_id=(to_a, to_b),
            device_id_type=MESH,
        ).start()

    near = [(b + n) % NPY for n in range(NPY)]

    @pl.loop(1, NPX)
    def _(d):
        for to_b in near:
            send_wall((a + d) % NPX, to_b)

    for to_b in near[1:]:
        send_wall(a, to_b)
    pltpu.make_async_copy(wsend.at[me], wrecv.at[me], rw.at[0]).start()

    got_half(0)
    pass_y(0)
    wait_bytes(wrecv, rw.at[0])
    arrived = wrecv[...].astype(F32).reshape(SLOTS, YB).astype(BF)
    source = jnp.dot(select[...], arrived, preferred_element_type=F32)
    s_ext[HALO : HALO + XB, YB : 2 * YB] = source * (source_gain * wall_gain)

    halo(s_ext, HALO, s_ext, sh.at[2], rh.at[2])
    got_half(2)
    pass_y(2)
    halo_wait(s_ext, sh.at[2], rh.at[2], False)

    heat = jnp.where(inside, s_ext[...], 0.0)
    temp = t_ext[...]
    for _ in range(COND_STEPS):
        new = coef[0] * temp + heat
        for n, side in enumerate(sides):
            new = new + coef[1 + n] * side(temp)
        temp = new
    solid[...] = temp[HALO : HALO + XB, YB : 2 * YB]
    keep_solid = pltpu.make_async_copy(solid, solid_out, load_sem.at[0])
    keep_solid.start()

    for f in range(3):
        wait_bytes(out.at[f], r4.at[f])
    keep_theta.wait()
    keep_solid.wait()
    for f in range(F):
        wait_bytes(xrows.at[f, pl.ds(0, XB * (NPX - 1))], s1.at[f])

        @pl.when(is_self)
        def _():
            wait_bytes(half.at[f, pl.ds(0, XB * (NPX - 1))], s2.at[f])

        @pl.when(jnp.logical_not(is_self))
        def _():
            wait_bytes(half.at[f], s2.at[f])

        wait_bytes(ysend.at[f, pl.ds(0, NPY - 1)], s4.at[f])
    wait_bytes(wsend.at[pl.ds(0, DEV - 1)], sw.at[0])
    wait_bytes(tsend.at[pl.ds(0, (NPY - 1) * 8)], sw.at[2])
    wait_bytes(tturn.at[pl.ds(0, (NPX - 1) * 8)], sw.at[3])


def finish(fields_in, solid_in, fields_out, solid_out, held, solid, sem_in, sem_out):
    pieces = [
        (fields_in.at[f], held.at[f], fields_out.at[f]) for f in range(F)
    ] + [(solid_in, solid, solid_out)]
    loads = [
        pltpu.make_async_copy(src, mid, sem_in.at[n])
        for n, (src, mid, _) in enumerate(pieces)
    ]
    stores = [
        pltpu.make_async_copy(mid, dst, sem_out.at[n])
        for n, (_, mid, dst) in enumerate(pieces)
    ]
    for load in loads:
        load.start()
    for load, store in zip(loads, stores):
        load.wait()
        store.start()
    for store in stores:
        store.wait()


def on_device(
    fields,
    x_operators,
    y_operators,
    viscosity,
    wall_tile,
    wall_owner,
    wall_row,
    solid_temp,
    conductivity,
):
    hbm = pl.BlockSpec(memory_space=pltpu.HBM)
    dma = pltpu.SemaphoreType.DMA
    new_fields, new_solid = pl.pallas_call(
        kernel,
        out_shape=(
            jax.ShapeDtypeStruct(fields.shape, BF),
            jax.ShapeDtypeStruct(solid_temp.shape, F32),
        ),
        in_specs=[hbm] * 9,
        out_specs=(hbm, hbm),
        scratch_shapes=[
            pltpu.SMEM((F,), F32),
            pltpu.VMEM((1, YB), jnp.int32),
            pltpu.VMEM((1, YB), jnp.int32),
            pltpu.VMEM((1, YB), jnp.int32),
            pltpu.VMEM((XB, YB), F32),
            pltpu.VMEM((3, NPX * XB, NPX * XB), BF),
            pltpu.VMEM((3, NPY * YB, NPY * YB), BF),
            pltpu.VMEM((3, NPY * YB, NPY * YB), BF),
            pltpu.VMEM((2, NPX * XB, NPX * XB), BF),
            pltpu.VMEM((NPY * YB, NPY * YB), BF),
            pltpu.VMEM((F, NPX * XB, YB), BF),
            pltpu.VMEM((F, NPX * XB, YB), BF),
            pltpu.VMEM((F, NPY, 2 * XB, YB), BF),
            pltpu.VMEM((F, NPY, 2, XB, YB), BF),
            pltpu.VMEM((NZ, XB, YB), BF),
            pltpu.VMEM((YB, NZ * XB), BF),
            pltpu.VMEM((SLOTS, YB), BF),
            pltpu.VMEM((XB, SLOTS), BF),
            pltpu.VMEM((NPY * 8, YB), BF),
            pltpu.VMEM((NPY * 8, YB), BF),
            pltpu.VMEM((NPX * 8, YB), BF),
            pltpu.VMEM((NPX * 8, YB), BF),
            pltpu.VMEM((DEV, CAP, YB), BF),
            pltpu.VMEM((DEV, CAP, YB), BF),
            pltpu.VMEM((ROWS, COLS), F32),
            pltpu.VMEM((ROWS, COLS), F32),
            pltpu.VMEM((ROWS, COLS), F32),
            pltpu.VMEM((5, ROWS, COLS), F32),
            dma((6,)),
            dma((F,)),
            dma((F,)),
            dma((F,)),
            dma((F,)),
            dma((F,)),
            dma((F,)),
            dma((4,)),
            dma((4,)),
            dma((3,)),
            dma((3,)),
            dma,
            pltpu.SemaphoreType.REGULAR,
        ],
        compiler_params=pltpu.CompilerParams(
            collective_id=0, has_side_effects=True, vmem_limit_bytes=67_043_328
        ),
        name="substep",
    )(
        fields,
        x_operators,
        y_operators,
        viscosity,
        wall_tile.reshape(1, -1),
        wall_owner.reshape(1, -1),
        wall_row.reshape(1, -1),
        solid_temp,
        conductivity,
    )
    return pl.pallas_call(
        finish,
        out_shape=(
            jax.ShapeDtypeStruct(fields.shape, BF),
            jax.ShapeDtypeStruct(solid_temp.shape, F32),
        ),
        in_specs=[hbm] * 2,
        out_specs=(hbm, hbm),
        scratch_shapes=[
            pltpu.VMEM((F, NZ, XB, YB), BF),
            pltpu.VMEM((XB, YB), F32),
            dma((F + 1,)),
            dma((F + 1,)),
        ],
        compiler_params=pltpu.CompilerParams(vmem_limit_bytes=67_043_328),
        name="finish",
    )(new_fields, new_solid)


def solution(mesh):
    return jax.shard_map(
        on_device,
        mesh=mesh,
        in_specs=(
            P(None, None, "px", "py"),
            P(),
            P(),
            P(),
            P(("px", "py")),
            P(("px", "py"), None),
            P(("px", "py")),
            P("px", "py"),
            P("px", "py"),
        ),
        out_specs=(P(None, None, "px", "py"), P("px", "py")),
        check_vma=False,
    )
```

```python
import jax
import jax.numpy as jnp
from jax import lax
from jax.experimental import pallas as pl
from jax.experimental.pallas import tpu as pltpu
from jax.sharding import PartitionSpec as P

COND_STEPS = 8
time_step = 0.25
wall_gain = 0.5
diffusion_rate = 0.24
source_gain = 0.1

NPX = 16
NPY = 8
DEV = NPX * NPY
F = 4
NZ = 16
XB = 64
YB = 128
CAP = 4
PIECES = 16
LINES = NPX * CAP
SLOTS = DEV * CAP
HALO = 8
ROWS = XB + 2 * HALO
COLS = 3 * YB
TILE = 256
MESH = pl.DeviceIdType.MESH
BF = jnp.bfloat16
F32 = jnp.float32


def iota(shape, axis):
    return lax.broadcasted_iota(jnp.int32, shape, axis)


def kernel(
    fields,
    xop_hbm,
    yop_hbm,
    visc_hbm,
    tile_hbm,
    owner_hbm,
    row_hbm,
    temp_hbm,
    cond_hbm,
    out,
    solid_out,
    visc,
    tile_ref,
    owner_ref,
    row_ref,
    solid,
    xop,
    yop,
    yopt,
    xsum,
    ysum,
    xrows,
    half,
    yrows,
    ysend,
    theta,
    gather,
    place,
    select,
    tsend,
    tmid,
    tturn,
    ttag,
    wsend,
    wrecv,
    t_ext,
    k_ext,
    s_ext,
    coef,
    load_sem,
    s1,
    r1,
    s2,
    r2,
    s4,
    r4,
    sw,
    rw,
    sh,
    rh,
    copy_sem,
    all_in,
):
    a = lax.axis_index("px")
    b = lax.axis_index("py")
    me = a * NPY + b
    held = a // 2
    par = a % 2
    is_self = held == b

    bar = pltpu.get_barrier_semaphore()

    @pl.loop(1, NPX)
    def _(d):
        pl.semaphore_signal(
            bar, inc=1, device_id=((a + d) % NPX, b), device_id_type=MESH
        )

    @pl.loop(1, NPY)
    def _(d):
        pl.semaphore_signal(
            bar, inc=1, device_id=(a, (b + d) % NPY), device_id_type=MESH
        )

    xload = pltpu.make_async_copy(xop_hbm, xop, load_sem.at[0])
    yload = pltpu.make_async_copy(yop_hbm, yop, load_sem.at[1])
    small = [
        pltpu.make_async_copy(src, dst, load_sem.at[2 + n])
        for n, (src, dst) in enumerate(
            (
                (visc_hbm, visc),
                (tile_hbm, tile_ref),
                (owner_hbm, owner_ref),
                (row_hbm, row_ref),
            )
        )
    ]
    for load in small:
        load.start()
    xload.start()
    yload.start()

    pl.semaphore_wait(bar, NPX + NPY - 2)

    def send_x(f):
        @pl.loop(1, NPX)
        def _(d):
            t = (a + d) % NPX
            pltpu.make_async_remote_copy(
                src_ref=fields.at[f, t],
                dst_ref=xrows.at[f, pl.ds(a * XB, XB)],
                send_sem=s1.at[f],
                recv_sem=r1.at[f],
                device_id=(t, b),
                device_id_type=MESH,
            ).start()

        pltpu.make_async_copy(
            fields.at[f, a], xrows.at[f, pl.ds(a * XB, XB)], r1.at[f]
        ).start()

    def wait_bytes(ref, sem):
        pltpu.make_async_copy(ref, ref, sem).wait()

    send_x(0)

    @pl.loop(1, NPX)
    def _(d):
        pl.semaphore_signal(
            all_in, inc=1, device_id=((a + d) % NPX, b), device_id_type=MESH
        )

    send_x(1)
    send_x(3)

    for load in small:
        load.wait()
    own = jnp.broadcast_to(owner_ref[...], (YB, YB))
    match = own == iota((YB, YB), 0)
    upper = (iota((YB, YB), 0) < iota((YB, YB), 1)).astype(F32).astype(BF)
    onehot = match.astype(F32)
    earlier = jnp.dot(onehot.astype(BF), upper, preferred_element_type=F32)
    pos = jnp.sum(earlier * onehot, axis=0, keepdims=True)
    owner = owner_ref[...]
    to_a = (owner // NPY).astype(F32) * CAP + pos
    to_b = (owner % NPY).astype(F32)
    dest = owner.astype(F32) * CAP + pos
    place[...] = (iota((SLOTS, YB), 0).astype(F32) == dest).astype(F32).astype(BF)
    name = row_ref[...].astype(F32) + 1.0
    named = jnp.where(
        (iota((NPY * 8, YB), 0) // 8).astype(F32) == to_b, name, 0.0
    ).astype(BF)
    spot = (iota((YB, YB), 0).astype(F32) == to_a).astype(F32).astype(BF)
    tsend[...] = lax.dot_general(
        named, spot, (((1,), (1,)), ((), ())), preferred_element_type=F32
    ).astype(BF)

    def along_y(src, dst, size, n):
        @pl.loop(1, NPY)
        def _(d):
            t = (b + d) % NPY
            pltpu.make_async_remote_copy(
                src_ref=src.at[pl.ds(t * size, size)],
                dst_ref=dst.at[pl.ds(b * size, size)],
                send_sem=sw.at[n],
                recv_sem=rw.at[n],
                device_id=(a, t),
                device_id_type=MESH,
            ).start()

        pltpu.make_async_copy(
            src.at[pl.ds(b * size, size)], dst.at[pl.ds(b * size, size)], rw.at[n]
        ).start()

    def along_x(src, dst, size, n):
        @pl.loop(1, NPX)
        def _(d):
            t = (a + d) % NPX
            pltpu.make_async_remote_copy(
                src_ref=src.at[pl.ds(t * size, size)],
                dst_ref=dst.at[pl.ds(a * size, size)],
                send_sem=sw.at[n],
                recv_sem=rw.at[n],
                device_id=(t, b),
                device_id_type=MESH,
            ).start()

        pltpu.make_async_copy(
            src.at[pl.ds(a * size, size)], dst.at[pl.ds(a * size, size)], rw.at[n]
        ).start()

    along_y(tsend, tmid, 8, 2)
    tcol = jnp.broadcast_to(tile_ref[...].astype(F32), (YB, YB)).T
    for n in range(NZ * XB // YB):
        gather[:, n * YB : (n + 1) * YB] = (
            (tcol == (iota((YB, YB), 1) + n * YB).astype(F32)).astype(F32).astype(BF)
        )

    pl.semaphore_wait(all_in, NPX - 1)

    def around():
        for dr in (-1, 0, 1):
            for dc in (-1, 0, 1):
                if dr or dc:
                    yield dr, dc

    def halo(src, r0, dst, ssem, rsem):
        for dr, dc in around():
            if dr == 0:
                rows, to = pl.ds(r0, XB), pl.ds(HALO, XB)
            elif dr == 1:
                rows, to = pl.ds(r0 + XB - HALO, HALO), pl.ds(0, HALO)
            else:
                rows, to = pl.ds(r0, HALO), pl.ds(HALO + XB, HALO)
            cols = pl.ds((1 - dc) * YB, YB)
            view = src.at[rows] if r0 == 0 else src.at[rows, pl.ds(YB, YB)]
            pltpu.make_async_remote_copy(
                src_ref=view,
                dst_ref=dst.at[to, cols],
                send_sem=ssem,
                recv_sem=rsem,
                device_id=((a + dr + NPX) % NPX, (b + dc + NPY) % NPY),
                device_id_type=MESH,
            ).start()

    def halo_wait(dst, ssem, rsem, own_block):
        amount = 6 * HALO + 2 * XB
        flat = xrows.at[0, pl.ds(0, 2 * amount)]
        wait_bytes(flat, ssem)
        if own_block:
            amount += XB
        wait_bytes(xrows.at[0, pl.ds(0, 2 * amount)], rsem)

    centre = (pl.ds(HALO, XB), pl.ds(YB, YB))
    halo(temp_hbm, 0, t_ext, sh.at[0], rh.at[0])
    halo(cond_hbm, 0, k_ext, sh.at[1], rh.at[1])
    pltpu.make_async_copy(temp_hbm, t_ext.at[centre], rh.at[0]).start()
    pltpu.make_async_copy(cond_hbm, k_ext.at[centre], rh.at[1]).start()

    def send_half(f, tile):
        @pl.loop(0, TILE // XB)
        def _(j):
            t = tile * (TILE // XB) + j
            src = half.at[f, pl.ds(t * XB, XB)]
            dst = yrows.at[f, b, pl.ds(par * XB, XB)]
            local = jnp.logical_and(is_self, t == a)

            @pl.when(local)
            def _():
                pltpu.make_async_copy(src, dst, r2.at[f]).start()

            @pl.when(jnp.logical_not(local))
            def _():
                pltpu.make_async_remote_copy(
                    src_ref=src,
                    dst_ref=dst,
                    send_sem=s2.at[f],
                    recv_sem=r2.at[f],
                    device_id=(t, held),
                    device_id_type=MESH,
                ).start()

    def tile_x(f, tile):
        rr = pl.ds(pl.multiple_of(tile * TILE, TILE), TILE)
        q = xrows[f]
        r0 = jnp.dot(xop[0, rr, :], q, preferred_element_type=F32)
        speed = xrows[0, rr, :].astype(F32)
        if f in (1, 3):
            rest = jnp.dot(xsum[f // 2, rr, :], q, preferred_element_type=F32)
            half[f, rr, :] = (rest - time_step * (speed * r0)).astype(BF)
        else:
            r1_ = jnp.dot(xop[1, rr, :], q, preferred_element_type=F32)
            r2_ = jnp.dot(xop[2, rr, :], q, preferred_element_type=F32)
            half[f, rr, :] = (
                r2_ + time_step * (-speed * r0 + visc[f] * r1_)
            ).astype(BF)

    tiles = NPX * XB // TILE

    def far_first(i):
        return (2 - i) * (1 - i // 2) + 3 * (3 - i) * (i // 2)


    def pass_x(f):
        def turn(i):
            return (a // 4 + far_first(i)) % tiles

        tile_x(f, turn(0))

        @pl.loop(1, tiles)
        def _(i):
            tile_x(f, turn(i))
            send_half(f, turn(i - 1))

        send_half(f, turn(tiles - 1))

    def send_y(f, tile):
        for j in range(TILE // YB):
            t = tile * (TILE // YB) + j
            src = ysend.at[f, t]
            if f == 3:
                dst = theta.at[pl.ds(2 * b, 2)]
            else:
                dst = out.at[f, pl.ds(2 * b, 2)]

            @pl.when(t == b)
            def _():
                pltpu.make_async_copy(src, dst, r4.at[f]).start()

            @pl.when(t != b)
            def _():
                pltpu.make_async_remote_copy(
                    src_ref=src,
                    dst_ref=dst,
                    send_sem=s4.at[f],
                    recv_sem=r4.at[f],
                    device_id=(a, t),
                    device_id_type=MESH,
                ).start()

    def tile_y(f, tile):
        rr = pl.ds(pl.multiple_of(tile * TILE, TILE), TILE)
        q = jnp.concatenate([yrows[f, n] for n in range(NPY)], axis=1)
        r0 = jnp.dot(q, yopt[0, :, rr], preferred_element_type=F32)
        r1_ = jnp.dot(q, yopt[1, :, rr], preferred_element_type=F32)
        r2_ = jnp.dot(q, yopt[2, :, rr], preferred_element_type=F32)
        for j in range(TILE // YB):
            t = tile * (TILE // YB) + j
            cc = slice(j * YB, (j + 1) * YB)
            speed = yrows[1, t].astype(F32)
            new = r2_[:, cc] + time_step * (
                -speed * r0[:, cc] + visc[f] * r1_[:, cc]
            )
            ysend[f, t] = new.astype(BF).reshape(2, XB, YB)

    ytiles = NPY * YB // TILE

    def pass_y(f):
        def turn(i):
            return (b // 2 + far_first(i)) % ytiles

        tile_y(f, turn(0))

        @pl.loop(1, ytiles)
        def _(i):
            tile_y(f, turn(i))
            send_y(f, turn(i - 1))

        send_y(f, turn(ytiles - 1))

    def got_x(f):
        wait_bytes(xrows.at[f], r1.at[f])

    def got_half(f):
        wait_bytes(yrows.at[f], r2.at[f])

    yload.wait()

    @pl.loop(0, NPY * YB // TILE)
    def _(n):
        rr = pl.ds(pl.multiple_of(n * TILE, TILE), TILE)
        for k in range(3):
            for j in range(NPY * YB // TILE):
                cc = slice(j * TILE, (j + 1) * TILE)
                yopt[k, cc, rr] = yop[k, rr, cc].T

    wait_bytes(tmid, rw.at[2])
    lane = iota((NPY * 8, YB), 1)
    from_b = iota((NPY * 8, YB), 0)
    pick = (from_b == ((lane % 32) // CAP) * 8) & (lane // 32 == a % 4)
    cross = lax.dot_general(
        tmid[...],
        pick.astype(F32).astype(BF),
        (((0,), (0,)), ((), ())),
        preferred_element_type=F32,
    )
    same = iota((YB, YB), 0) % CAP == iota((YB, YB), 1) % CAP
    group = iota((YB, YB), 0) // 8 == iota((YB, YB), 1) // CAP
    tturn[...] = jnp.dot(
        group.astype(F32).astype(BF),
        jnp.where(same, cross, 0.0).astype(BF),
        preferred_element_type=F32,
    ).astype(BF)
    along_x(tturn, ttag, 8, 3)

    xload.wait()

    @pl.loop(0, NPX * XB // 32)
    def _(n):
        rr = pl.ds(pl.multiple_of(n * 32, 32), 32)
        second = time_step * xop[1, rr, :].astype(F32)
        smooth = xop[2, rr, :].astype(F32)
        xsum[0, rr, :] = (smooth + visc[1] * second).astype(BF)
        xsum[1, rr, :] = (smooth + visc[3] * second).astype(BF)

    got_x(0)
    got_x(1)
    pass_x(1)
    got_x(3)
    pass_x(3)
    pass_x(0)
    send_x(2)

    wait_bytes(ttag, rw.at[3])
    for n in range(SLOTS // YB):
        tag = jnp.zeros((8, YB), F32)
        for k in range(4):
            tag = tag + ttag[(4 * n + k) * 8 : (4 * n + k + 1) * 8, :].astype(F32)
        select[:, n * YB : (n + 1) * YB] = (
            (jnp.broadcast_to(tag[:1], (XB, YB)) == (iota((XB, YB), 0) + 1).astype(F32))
            .astype(F32)
            .astype(BF)
        )

    halo_wait(t_ext, sh.at[0], rh.at[0], True)
    halo_wait(k_ext, sh.at[1], rh.at[1], True)
    grow = iota((ROWS, COLS), 0) + (a * XB - HALO)
    gcol = iota((ROWS, COLS), 1) + (b * YB - YB)
    inside = (
        (grow >= 0) & (grow < NPX * XB) & (gcol >= 0) & (gcol < NPY * YB)
    )
    kappa = jnp.where(inside, k_ext[...], 0.0)
    t_ext[...] = jnp.where(inside, t_ext[...], 0.0)

    def north(v):
        return pltpu.roll(v, 1, 0)

    def south(v):
        return pltpu.roll(v, ROWS - 1, 0)

    def west(v):
        return pltpu.roll(v, 1, 1)

    def east(v):
        return pltpu.roll(v, COLS - 1, 1)

    rate = 0.5 * diffusion_rate
    sides = (north, south, west, east)
    total = jnp.zeros((ROWS, COLS), F32)
    for n, side in enumerate(sides):
        part = jnp.where(inside, rate * (kappa + side(kappa)), 0.0)
        coef[1 + n] = part
        total = total + part
    coef[0] = 1.0 - total


    got_half(1)
    got_half(3)
    pass_y(3)
    pass_y(1)
    got_x(2)
    pass_x(2)
    wait_bytes(theta, r4.at[3])
    keep_theta = pltpu.make_async_copy(theta, out.at[3], copy_sem)
    keep_theta.start()
    lines = theta[...].reshape(NZ * XB, YB)
    flux = jnp.dot(gather[...], lines, preferred_element_type=F32).astype(BF)
    wsend[...] = (
        jnp.dot(place[...], flux, preferred_element_type=F32)
        .reshape(DEV, CAP, YB)
        .astype(BF)
    )

    def send_wall(to_a, to_b):
        pltpu.make_async_remote_copy(
            src_ref=wsend.at[to_a * NPY + to_b],
            dst_ref=wrecv.at[me],
            send_sem=sw.at[0],
            recv_sem=rw.at[0],
            device_id=(to_a, to_b),
            device_id_type=MESH,
        ).start()

    near = [(b + n) % NPY for n in range(NPY)]

    @pl.loop(1, NPX)
    def _(d):
        for to_b in near:
            send_wall((a + d) % NPX, to_b)

    for to_b in near[1:]:
        send_wall(a, to_b)
    pltpu.make_async_copy(wsend.at[me], wrecv.at[me], rw.at[0]).start()

    got_half(0)
    pass_y(0)
    wait_bytes(wrecv, rw.at[0])
    arrived = wrecv[...].astype(F32).reshape(SLOTS, YB).astype(BF)
    source = jnp.dot(select[...], arrived, preferred_element_type=F32)
    s_ext[HALO : HALO + XB, YB : 2 * YB] = source * (source_gain * wall_gain)

    halo(s_ext, HALO, s_ext, sh.at[2], rh.at[2])
    got_half(2)
    pass_y(2)
    halo_wait(s_ext, sh.at[2], rh.at[2], False)

    heat = jnp.where(inside, s_ext[...], 0.0)
    temp = t_ext[...]
    for _ in range(COND_STEPS):
        new = coef[0] * temp + heat
        for n, side in enumerate(sides):
            new = new + coef[1 + n] * side(temp)
        temp = new
    solid[...] = temp[HALO : HALO + XB, YB : 2 * YB]
    keep_solid = pltpu.make_async_copy(solid, solid_out, load_sem.at[0])
    keep_solid.start()

    for f in range(3):
        wait_bytes(out.at[f], r4.at[f])
    keep_theta.wait()
    keep_solid.wait()
    for f in range(F):
        wait_bytes(xrows.at[f, pl.ds(0, XB * (NPX - 1))], s1.at[f])

        @pl.when(is_self)
        def _():
            wait_bytes(half.at[f, pl.ds(0, XB * (NPX - 1))], s2.at[f])

        @pl.when(jnp.logical_not(is_self))
        def _():
            wait_bytes(half.at[f], s2.at[f])

        wait_bytes(ysend.at[f, pl.ds(0, NPY - 1)], s4.at[f])
    wait_bytes(wsend.at[pl.ds(0, DEV - 1)], sw.at[0])
    wait_bytes(tsend.at[pl.ds(0, (NPY - 1) * 8)], sw.at[2])
    wait_bytes(tturn.at[pl.ds(0, (NPX - 1) * 8)], sw.at[3])


def finish(fields_in, solid_in, fields_out, solid_out, held, solid, sem_in, sem_out):
    part = NZ * F // PIECES
    pieces = [(solid_in, solid, solid_out)]
    for n in range(PIECES):
        f, layers = n * part // NZ, pl.ds(n * part % NZ, part)
        pieces.append(
            (fields_in.at[f, layers], held.at[f, layers], fields_out.at[f, layers])
        )
    loads = [
        pltpu.make_async_copy(src, mid, sem_in.at[n])
        for n, (src, mid, _) in enumerate(pieces)
    ]
    stores = [
        pltpu.make_async_copy(mid, dst, sem_out.at[n])
        for n, (_, mid, dst) in enumerate(pieces)
    ]
    for load in loads:
        load.start()
    for load, store in zip(loads, stores):
        load.wait()
        store.start()
    for store in stores:
        store.wait()


def on_device(
    fields,
    x_operators,
    y_operators,
    viscosity,
    wall_tile,
    wall_owner,
    wall_row,
    solid_temp,
    conductivity,
):
    hbm = pl.BlockSpec(memory_space=pltpu.HBM)
    dma = pltpu.SemaphoreType.DMA
    new_fields, new_solid = pl.pallas_call(
        kernel,
        out_shape=(
            jax.ShapeDtypeStruct(fields.shape, BF),
            jax.ShapeDtypeStruct(solid_temp.shape, F32),
        ),
        in_specs=[hbm] * 9,
        out_specs=(hbm, hbm),
        scratch_shapes=[
            pltpu.SMEM((F,), F32),
            pltpu.VMEM((1, YB), jnp.int32),
            pltpu.VMEM((1, YB), jnp.int32),
            pltpu.VMEM((1, YB), jnp.int32),
            pltpu.VMEM((XB, YB), F32),
            pltpu.VMEM((3, NPX * XB, NPX * XB), BF),
            pltpu.VMEM((3, NPY * YB, NPY * YB), BF),
            pltpu.VMEM((3, NPY * YB, NPY * YB), BF),
            pltpu.VMEM((2, NPX * XB, NPX * XB), BF),
            pltpu.VMEM((NPY * YB, NPY * YB), BF),
            pltpu.VMEM((F, NPX * XB, YB), BF),
            pltpu.VMEM((F, NPX * XB, YB), BF),
            pltpu.VMEM((F, NPY, 2 * XB, YB), BF),
            pltpu.VMEM((F, NPY, 2, XB, YB), BF),
            pltpu.VMEM((NZ, XB, YB), BF),
            pltpu.VMEM((YB, NZ * XB), BF),
            pltpu.VMEM((SLOTS, YB), BF),
            pltpu.VMEM((XB, SLOTS), BF),
            pltpu.VMEM((NPY * 8, YB), BF),
            pltpu.VMEM((NPY * 8, YB), BF),
            pltpu.VMEM((NPX * 8, YB), BF),
            pltpu.VMEM((NPX * 8, YB), BF),
            pltpu.VMEM((DEV, CAP, YB), BF),
            pltpu.VMEM((DEV, CAP, YB), BF),
            pltpu.VMEM((ROWS, COLS), F32),
            pltpu.VMEM((ROWS, COLS), F32),
            pltpu.VMEM((ROWS, COLS), F32),
            pltpu.VMEM((5, ROWS, COLS), F32),
            dma((6,)),
            dma((F,)),
            dma((F,)),
            dma((F,)),
            dma((F,)),
            dma((F,)),
            dma((F,)),
            dma((4,)),
            dma((4,)),
            dma((3,)),
            dma((3,)),
            dma,
            pltpu.SemaphoreType.REGULAR,
        ],
        compiler_params=pltpu.CompilerParams(
            collective_id=0, has_side_effects=True, vmem_limit_bytes=67_043_328
        ),
        name="substep",
    )(
        fields,
        x_operators,
        y_operators,
        viscosity,
        wall_tile.reshape(1, -1),
        wall_owner.reshape(1, -1),
        wall_row.reshape(1, -1),
        solid_temp,
        conductivity,
    )
    return pl.pallas_call(
        finish,
        out_shape=(
            jax.ShapeDtypeStruct(fields.shape, BF),
            jax.ShapeDtypeStruct(solid_temp.shape, F32),
        ),
        in_specs=[hbm] * 2,
        out_specs=(hbm, hbm),
        scratch_shapes=[
            pltpu.VMEM((F, NZ, XB, YB), BF),
            pltpu.VMEM((XB, YB), F32),
            dma((PIECES + 1,)),
            dma((PIECES + 1,)),
        ],
        compiler_params=pltpu.CompilerParams(vmem_limit_bytes=67_043_328),
        name="finish",
    )(new_fields, new_solid)


def solution(mesh):
    return jax.shard_map(
        on_device,
        mesh=mesh,
        in_specs=(
            P(None, None, "px", "py"),
            P(),
            P(),
            P(),
            P(("px", "py")),
            P(("px", "py"), None),
            P(("px", "py")),
            P("px", "py"),
            P("px", "py"),
        ),
        out_specs=(P(None, None, "px", "py"), P("px", "py")),
        check_vma=False,
    )
```

```python
import jax
import jax.numpy as jnp
from jax import lax
from jax.experimental import pallas as pl
from jax.experimental.pallas import tpu as pltpu
from jax.sharding import PartitionSpec as P

COND_STEPS = 8
time_step = 0.25
wall_gain = 0.5
diffusion_rate = 0.24
source_gain = 0.1

NPX = 16
NPY = 8
DEV = NPX * NPY
F = 4
NZ = 16
XB = 64
YB = 128
CAP = 4
LINES = NPX * CAP
SLOTS = DEV * CAP
HALO = 8
ROWS = XB + 2 * HALO
COLS = 3 * YB
TILE = 256
MESH = pl.DeviceIdType.MESH
BF = jnp.bfloat16
F32 = jnp.float32


def iota(shape, axis):
    return lax.broadcasted_iota(jnp.int32, shape, axis)


def kernel(
    fields,
    xop_hbm,
    yop_hbm,
    visc_hbm,
    tile_hbm,
    owner_hbm,
    row_hbm,
    temp_hbm,
    cond_hbm,
    out,
    solid_out,
    visc,
    tile_ref,
    owner_ref,
    row_ref,
    solid,
    xop,
    yop,
    yopt,
    xsum,
    ysum,
    xrows,
    half,
    yrows,
    ysend,
    theta,
    gather,
    place,
    select,
    tsend,
    tmid,
    tturn,
    ttag,
    wsend,
    wrecv,
    t_ext,
    k_ext,
    s_ext,
    coef,
    load_sem,
    s1,
    r1,
    s2,
    r2,
    s4,
    r4,
    sw,
    rw,
    sh,
    rh,
    copy_sem,
    all_in,
):
    a = lax.axis_index("px")
    b = lax.axis_index("py")
    me = a * NPY + b
    held = a // 2
    par = a % 2
    is_self = held == b

    bar = pltpu.get_barrier_semaphore()

    @pl.loop(1, NPX)
    def _(d):
        pl.semaphore_signal(
            bar, inc=1, device_id=((a + d) % NPX, b), device_id_type=MESH
        )

    @pl.loop(1, NPY)
    def _(d):
        pl.semaphore_signal(
            bar, inc=1, device_id=(a, (b + d) % NPY), device_id_type=MESH
        )

    xload = pltpu.make_async_copy(xop_hbm, xop, load_sem.at[0])
    yload = pltpu.make_async_copy(yop_hbm, yop, load_sem.at[1])
    small = [
        pltpu.make_async_copy(src, dst, load_sem.at[2 + n])
        for n, (src, dst) in enumerate(
            (
                (visc_hbm, visc),
                (tile_hbm, tile_ref),
                (owner_hbm, owner_ref),
                (row_hbm, row_ref),
            )
        )
    ]
    for load in small:
        load.start()
    xload.start()
    yload.start()

    pl.semaphore_wait(bar, NPX + NPY - 2)

    def send_x(f):
        @pl.loop(1, NPX)
        def _(d):
            t = (a + d) % NPX
            pltpu.make_async_remote_copy(
                src_ref=fields.at[f, t],
                dst_ref=xrows.at[f, pl.ds(a * XB, XB)],
                send_sem=s1.at[f],
                recv_sem=r1.at[f],
                device_id=(t, b),
                device_id_type=MESH,
            ).start()

        pltpu.make_async_copy(
            fields.at[f, a], xrows.at[f, pl.ds(a * XB, XB)], r1.at[f]
        ).start()

    def wait_bytes(ref, sem):
        pltpu.make_async_copy(ref, ref, sem).wait()

    send_x(0)

    @pl.loop(1, NPX)
    def _(d):
        pl.semaphore_signal(
            all_in, inc=1, device_id=((a + d) % NPX, b), device_id_type=MESH
        )

    send_x(1)
    send_x(3)

    for load in small:
        load.wait()
    own = jnp.broadcast_to(owner_ref[...], (YB, YB))
    match = own == iota((YB, YB), 0)
    upper = (iota((YB, YB), 0) < iota((YB, YB), 1)).astype(F32).astype(BF)
    onehot = match.astype(F32)
    earlier = jnp.dot(onehot.astype(BF), upper, preferred_element_type=F32)
    pos = jnp.sum(earlier * onehot, axis=0, keepdims=True)
    owner = owner_ref[...]
    to_a = (owner // NPY).astype(F32) * CAP + pos
    to_b = (owner % NPY).astype(F32)
    dest = owner.astype(F32) * CAP + pos
    place[...] = (iota((SLOTS, YB), 0).astype(F32) == dest).astype(F32).astype(BF)
    name = row_ref[...].astype(F32) + 1.0
    named = jnp.where(
        (iota((NPY * 8, YB), 0) // 8).astype(F32) == to_b, name, 0.0
    ).astype(BF)
    spot = (iota((YB, YB), 0).astype(F32) == to_a).astype(F32).astype(BF)
    tsend[...] = lax.dot_general(
        named, spot, (((1,), (1,)), ((), ())), preferred_element_type=F32
    ).astype(BF)

    def along_y(src, dst, size, n):
        @pl.loop(1, NPY)
        def _(d):
            t = (b + d) % NPY
            pltpu.make_async_remote_copy(
                src_ref=src.at[pl.ds(t * size, size)],
                dst_ref=dst.at[pl.ds(b * size, size)],
                send_sem=sw.at[n],
                recv_sem=rw.at[n],
                device_id=(a, t),
                device_id_type=MESH,
            ).start()

        pltpu.make_async_copy(
            src.at[pl.ds(b * size, size)], dst.at[pl.ds(b * size, size)], rw.at[n]
        ).start()

    def along_x(src, dst, size, n):
        @pl.loop(1, NPX)
        def _(d):
            t = (a + d) % NPX
            pltpu.make_async_remote_copy(
                src_ref=src.at[pl.ds(t * size, size)],
                dst_ref=dst.at[pl.ds(a * size, size)],
                send_sem=sw.at[n],
                recv_sem=rw.at[n],
                device_id=(t, b),
                device_id_type=MESH,
            ).start()

        pltpu.make_async_copy(
            src.at[pl.ds(a * size, size)], dst.at[pl.ds(a * size, size)], rw.at[n]
        ).start()

    along_y(tsend, tmid, 8, 2)
    tcol = jnp.broadcast_to(tile_ref[...].astype(F32), (YB, YB)).T
    for n in range(NZ * XB // YB):
        gather[:, n * YB : (n + 1) * YB] = (
            (tcol == (iota((YB, YB), 1) + n * YB).astype(F32)).astype(F32).astype(BF)
        )

    pl.semaphore_wait(all_in, NPX - 1)

    def around():
        for dr in (-1, 0, 1):
            for dc in (-1, 0, 1):
                if dr or dc:
                    yield dr, dc

    def halo(src, r0, dst, ssem, rsem):
        for dr, dc in around():
            if dr == 0:
                rows, to = pl.ds(r0, XB), pl.ds(HALO, XB)
            elif dr == 1:
                rows, to = pl.ds(r0 + XB - HALO, HALO), pl.ds(0, HALO)
            else:
                rows, to = pl.ds(r0, HALO), pl.ds(HALO + XB, HALO)
            cols = pl.ds((1 - dc) * YB, YB)
            view = src.at[rows] if r0 == 0 else src.at[rows, pl.ds(YB, YB)]
            pltpu.make_async_remote_copy(
                src_ref=view,
                dst_ref=dst.at[to, cols],
                send_sem=ssem,
                recv_sem=rsem,
                device_id=((a + dr + NPX) % NPX, (b + dc + NPY) % NPY),
                device_id_type=MESH,
            ).start()

    def halo_wait(dst, ssem, rsem, own_block):
        amount = 6 * HALO + 2 * XB
        flat = xrows.at[0, pl.ds(0, 2 * amount)]
        wait_bytes(flat, ssem)
        if own_block:
            amount += XB
        wait_bytes(xrows.at[0, pl.ds(0, 2 * amount)], rsem)

    centre = (pl.ds(HALO, XB), pl.ds(YB, YB))
    halo(temp_hbm, 0, t_ext, sh.at[0], rh.at[0])
    halo(cond_hbm, 0, k_ext, sh.at[1], rh.at[1])
    pltpu.make_async_copy(temp_hbm, t_ext.at[centre], rh.at[0]).start()
    pltpu.make_async_copy(cond_hbm, k_ext.at[centre], rh.at[1]).start()

    def send_half(f, tile):
        @pl.loop(0, TILE // XB)
        def _(j):
            t = tile * (TILE // XB) + j
            src = half.at[f, pl.ds(t * XB, XB)]
            dst = yrows.at[f, b, pl.ds(par * XB, XB)]
            local = jnp.logical_and(is_self, t == a)

            @pl.when(local)
            def _():
                pltpu.make_async_copy(src, dst, r2.at[f]).start()

            @pl.when(jnp.logical_not(local))
            def _():
                pltpu.make_async_remote_copy(
                    src_ref=src,
                    dst_ref=dst,
                    send_sem=s2.at[f],
                    recv_sem=r2.at[f],
                    device_id=(t, held),
                    device_id_type=MESH,
                ).start()

    def tile_x(f, tile):
        rr = pl.ds(pl.multiple_of(tile * TILE, TILE), TILE)
        q = xrows[f]
        r0 = jnp.dot(xop[0, rr, :], q, preferred_element_type=F32)
        speed = xrows[0, rr, :].astype(F32)
        if f > 0:
            rest = jnp.dot(xsum[f - 1, rr, :], q, preferred_element_type=F32)
            half[f, rr, :] = (rest - time_step * (speed * r0)).astype(BF)
        else:
            r1_ = jnp.dot(xop[1, rr, :], q, preferred_element_type=F32)
            r2_ = jnp.dot(xop[2, rr, :], q, preferred_element_type=F32)
            half[f, rr, :] = (
                r2_ + time_step * (-speed * r0 + visc[f] * r1_)
            ).astype(BF)

    tiles = NPX * XB // TILE

    def far_first(i):
        return (2 - i) * (1 - i // 2) + 3 * (3 - i) * (i // 2)


    def pass_x(f):
        def turn(i):
            return (a // 4 + far_first(i)) % tiles

        tile_x(f, turn(0))

        @pl.loop(1, tiles)
        def _(i):
            tile_x(f, turn(i))
            send_half(f, turn(i - 1))

        send_half(f, turn(tiles - 1))

    def send_y(f, tile):
        for j in range(TILE // YB):
            t = tile * (TILE // YB) + j
            src = ysend.at[f, t]
            if f == 3:
                dst = theta.at[pl.ds(2 * b, 2)]
            else:
                dst = out.at[f, pl.ds(2 * b, 2)]

            @pl.when(t == b)
            def _():
                pltpu.make_async_copy(src, dst, r4.at[f]).start()

            @pl.when(t != b)
            def _():
                pltpu.make_async_remote_copy(
                    src_ref=src,
                    dst_ref=dst,
                    send_sem=s4.at[f],
                    recv_sem=r4.at[f],
                    device_id=(a, t),
                    device_id_type=MESH,
                ).start()

    def tile_y(f, tile):
        rr = pl.ds(pl.multiple_of(tile * TILE, TILE), TILE)
        q = jnp.concatenate([yrows[f, n] for n in range(NPY)], axis=1)
        r0 = jnp.dot(q, yopt[0, :, rr], preferred_element_type=F32)
        r1_ = jnp.dot(q, yopt[1, :, rr], preferred_element_type=F32)
        r2_ = jnp.dot(q, yopt[2, :, rr], preferred_element_type=F32)
        for j in range(TILE // YB):
            t = tile * (TILE // YB) + j
            cc = slice(j * YB, (j + 1) * YB)
            speed = yrows[1, t].astype(F32)
            new = r2_[:, cc] + time_step * (
                -speed * r0[:, cc] + visc[f] * r1_[:, cc]
            )
            ysend[f, t] = new.astype(BF).reshape(2, XB, YB)

    ytiles = NPY * YB // TILE

    def pass_y(f):
        def turn(i):
            return (b // 2 + far_first(i)) % ytiles

        tile_y(f, turn(0))

        @pl.loop(1, ytiles)
        def _(i):
            tile_y(f, turn(i))
            send_y(f, turn(i - 1))

        send_y(f, turn(ytiles - 1))

    def got_x(f):
        wait_bytes(xrows.at[f], r1.at[f])

    def got_half(f):
        wait_bytes(yrows.at[f], r2.at[f])

    yload.wait()

    @pl.loop(0, NPY * YB // TILE)
    def _(n):
        rr = pl.ds(pl.multiple_of(n * TILE, TILE), TILE)
        for k in range(3):
            for j in range(NPY * YB // TILE):
                cc = slice(j * TILE, (j + 1) * TILE)
                yopt[k, cc, rr] = yop[k, rr, cc].T

    wait_bytes(tmid, rw.at[2])
    lane = iota((NPY * 8, YB), 1)
    from_b = iota((NPY * 8, YB), 0)
    pick = (from_b == ((lane % 32) // CAP) * 8) & (lane // 32 == a % 4)
    cross = lax.dot_general(
        tmid[...],
        pick.astype(F32).astype(BF),
        (((0,), (0,)), ((), ())),
        preferred_element_type=F32,
    )
    same = iota((YB, YB), 0) % CAP == iota((YB, YB), 1) % CAP
    group = iota((YB, YB), 0) // 8 == iota((YB, YB), 1) // CAP
    tturn[...] = jnp.dot(
        group.astype(F32).astype(BF),
        jnp.where(same, cross, 0.0).astype(BF),
        preferred_element_type=F32,
    ).astype(BF)
    along_x(tturn, ttag, 8, 3)

    xload.wait()

    @pl.loop(0, NPX * XB // 32)
    def _(n):
        rr = pl.ds(pl.multiple_of(n * 32, 32), 32)
        second = time_step * xop[1, rr, :].astype(F32)
        smooth = xop[2, rr, :].astype(F32)
        xsum[0, rr, :] = (smooth + visc[1] * second).astype(BF)
        xsum[1, rr, :] = (smooth + visc[2] * second).astype(BF)
        xsum[2, rr, :] = (smooth + visc[3] * second).astype(BF)

    got_x(0)
    got_x(1)
    pass_x(1)
    got_x(3)
    pass_x(3)
    pass_x(0)
    send_x(2)

    wait_bytes(ttag, rw.at[3])
    for n in range(SLOTS // YB):
        tag = jnp.zeros((8, YB), F32)
        for k in range(4):
            tag = tag + ttag[(4 * n + k) * 8 : (4 * n + k + 1) * 8, :].astype(F32)
        select[:, n * YB : (n + 1) * YB] = (
            (jnp.broadcast_to(tag[:1], (XB, YB)) == (iota((XB, YB), 0) + 1).astype(F32))
            .astype(F32)
            .astype(BF)
        )

    halo_wait(t_ext, sh.at[0], rh.at[0], True)
    halo_wait(k_ext, sh.at[1], rh.at[1], True)
    grow = iota((ROWS, COLS), 0) + (a * XB - HALO)
    gcol = iota((ROWS, COLS), 1) + (b * YB - YB)
    inside = (
        (grow >= 0) & (grow < NPX * XB) & (gcol >= 0) & (gcol < NPY * YB)
    )
    kappa = jnp.where(inside, k_ext[...], 0.0)
    t_ext[...] = jnp.where(inside, t_ext[...], 0.0)

    def north(v):
        return pltpu.roll(v, 1, 0)

    def south(v):
        return pltpu.roll(v, ROWS - 1, 0)

    def west(v):
        return pltpu.roll(v, 1, 1)

    def east(v):
        return pltpu.roll(v, COLS - 1, 1)

    rate = 0.5 * diffusion_rate
    sides = (north, south, west, east)
    total = jnp.zeros((ROWS, COLS), F32)
    for n, side in enumerate(sides):
        part = jnp.where(inside, rate * (kappa + side(kappa)), 0.0)
        coef[1 + n] = part
        total = total + part
    coef[0] = 1.0 - total


    got_half(1)
    got_half(3)
    pass_y(3)
    pass_y(1)
    got_x(2)
    pass_x(2)
    wait_bytes(theta, r4.at[3])
    keep_theta = pltpu.make_async_copy(theta, out.at[3], copy_sem)
    keep_theta.start()
    lines = theta[...].reshape(NZ * XB, YB)
    flux = jnp.dot(gather[...], lines, preferred_element_type=F32).astype(BF)
    wsend[...] = (
        jnp.dot(place[...], flux, preferred_element_type=F32)
        .reshape(DEV, CAP, YB)
        .astype(BF)
    )

    def send_wall(to_a, to_b):
        pltpu.make_async_remote_copy(
            src_ref=wsend.at[to_a * NPY + to_b],
            dst_ref=wrecv.at[me],
            send_sem=sw.at[0],
            recv_sem=rw.at[0],
            device_id=(to_a, to_b),
            device_id_type=MESH,
        ).start()

    near = [(b + n) % NPY for n in range(NPY)]

    @pl.loop(1, NPX)
    def _(d):
        for to_b in near:
            send_wall((a + d) % NPX, to_b)

    for to_b in near[1:]:
        send_wall(a, to_b)
    pltpu.make_async_copy(wsend.at[me], wrecv.at[me], rw.at[0]).start()

    got_half(0)
    pass_y(0)
    wait_bytes(wrecv, rw.at[0])
    arrived = wrecv[...].astype(F32).reshape(SLOTS, YB).astype(BF)
    source = jnp.dot(select[...], arrived, preferred_element_type=F32)
    s_ext[HALO : HALO + XB, YB : 2 * YB] = source * (source_gain * wall_gain)

    halo(s_ext, HALO, s_ext, sh.at[2], rh.at[2])
    got_half(2)
    pass_y(2)
    halo_wait(s_ext, sh.at[2], rh.at[2], False)

    heat = jnp.where(inside, s_ext[...], 0.0)
    temp = t_ext[...]
    for _ in range(COND_STEPS):
        new = coef[0] * temp + heat
        for n, side in enumerate(sides):
            new = new + coef[1 + n] * side(temp)
        temp = new
    solid[...] = temp[HALO : HALO + XB, YB : 2 * YB]
    keep_solid = pltpu.make_async_copy(solid, solid_out, load_sem.at[0])
    keep_solid.start()

    for f in range(3):
        wait_bytes(out.at[f], r4.at[f])
    keep_theta.wait()
    keep_solid.wait()
    for f in range(F):
        wait_bytes(xrows.at[f, pl.ds(0, XB * (NPX - 1))], s1.at[f])

        @pl.when(is_self)
        def _():
            wait_bytes(half.at[f, pl.ds(0, XB * (NPX - 1))], s2.at[f])

        @pl.when(jnp.logical_not(is_self))
        def _():
            wait_bytes(half.at[f], s2.at[f])

        wait_bytes(ysend.at[f, pl.ds(0, NPY - 1)], s4.at[f])
    wait_bytes(wsend.at[pl.ds(0, DEV - 1)], sw.at[0])
    wait_bytes(tsend.at[pl.ds(0, (NPY - 1) * 8)], sw.at[2])
    wait_bytes(tturn.at[pl.ds(0, (NPX - 1) * 8)], sw.at[3])


def finish(fields_in, solid_in, fields_out, solid_out, held, solid, sem_in, sem_out):
    pieces = [
        (fields_in.at[f], held.at[f], fields_out.at[f]) for f in range(F)
    ] + [(solid_in, solid, solid_out)]
    loads = [
        pltpu.make_async_copy(src, mid, sem_in.at[n])
        for n, (src, mid, _) in enumerate(pieces)
    ]
    stores = [
        pltpu.make_async_copy(mid, dst, sem_out.at[n])
        for n, (_, mid, dst) in enumerate(pieces)
    ]
    for load in loads:
        load.start()
    for load, store in zip(loads, stores):
        load.wait()
        store.start()
    for store in stores:
        store.wait()


def on_device(
    fields,
    x_operators,
    y_operators,
    viscosity,
    wall_tile,
    wall_owner,
    wall_row,
    solid_temp,
    conductivity,
):
    hbm = pl.BlockSpec(memory_space=pltpu.HBM)
    dma = pltpu.SemaphoreType.DMA
    new_fields, new_solid = pl.pallas_call(
        kernel,
        out_shape=(
            jax.ShapeDtypeStruct(fields.shape, BF),
            jax.ShapeDtypeStruct(solid_temp.shape, F32),
        ),
        in_specs=[hbm] * 9,
        out_specs=(hbm, hbm),
        scratch_shapes=[
            pltpu.SMEM((F,), F32),
            pltpu.VMEM((1, YB), jnp.int32),
            pltpu.VMEM((1, YB), jnp.int32),
            pltpu.VMEM((1, YB), jnp.int32),
            pltpu.VMEM((XB, YB), F32),
            pltpu.VMEM((3, NPX * XB, NPX * XB), BF),
            pltpu.VMEM((3, NPY * YB, NPY * YB), BF),
            pltpu.VMEM((3, NPY * YB, NPY * YB), BF),
            pltpu.VMEM((3, NPX * XB, NPX * XB), BF),
            pltpu.VMEM((NPY * YB, NPY * YB), BF),
            pltpu.VMEM((F, NPX * XB, YB), BF),
            pltpu.VMEM((F, NPX * XB, YB), BF),
            pltpu.VMEM((F, NPY, 2 * XB, YB), BF),
            pltpu.VMEM((F, NPY, 2, XB, YB), BF),
            pltpu.VMEM((NZ, XB, YB), BF),
            pltpu.VMEM((YB, NZ * XB), BF),
            pltpu.VMEM((SLOTS, YB), BF),
            pltpu.VMEM((XB, SLOTS), BF),
            pltpu.VMEM((NPY * 8, YB), BF),
            pltpu.VMEM((NPY * 8, YB), BF),
            pltpu.VMEM((NPX * 8, YB), BF),
            pltpu.VMEM((NPX * 8, YB), BF),
            pltpu.VMEM((DEV, CAP, YB), BF),
            pltpu.VMEM((DEV, CAP, YB), BF),
            pltpu.VMEM((ROWS, COLS), F32),
            pltpu.VMEM((ROWS, COLS), F32),
            pltpu.VMEM((ROWS, COLS), F32),
            pltpu.VMEM((5, ROWS, COLS), F32),
            dma((6,)),
            dma((F,)),
            dma((F,)),
            dma((F,)),
            dma((F,)),
            dma((F,)),
            dma((F,)),
            dma((4,)),
            dma((4,)),
            dma((3,)),
            dma((3,)),
            dma,
            pltpu.SemaphoreType.REGULAR,
        ],
        compiler_params=pltpu.CompilerParams(
            collective_id=0, has_side_effects=True, vmem_limit_bytes=67_043_328
        ),
        name="substep",
    )(
        fields,
        x_operators,
        y_operators,
        viscosity,
        wall_tile.reshape(1, -1),
        wall_owner.reshape(1, -1),
        wall_row.reshape(1, -1),
        solid_temp,
        conductivity,
    )
    return pl.pallas_call(
        finish,
        out_shape=(
            jax.ShapeDtypeStruct(fields.shape, BF),
            jax.ShapeDtypeStruct(solid_temp.shape, F32),
        ),
        in_specs=[hbm] * 2,
        out_specs=(hbm, hbm),
        scratch_shapes=[
            pltpu.VMEM((F, NZ, XB, YB), BF),
            pltpu.VMEM((XB, YB), F32),
            dma((F + 1,)),
            dma((F + 1,)),
        ],
        compiler_params=pltpu.CompilerParams(vmem_limit_bytes=67_043_328),
        name="finish",
    )(new_fields, new_solid)


def solution(mesh):
    return jax.shard_map(
        on_device,
        mesh=mesh,
        in_specs=(
            P(None, None, "px", "py"),
            P(),
            P(),
            P(),
            P(("px", "py")),
            P(("px", "py"), None),
            P(("px", "py")),
            P("px", "py"),
            P("px", "py"),
        ),
        out_specs=(P(None, None, "px", "py"), P("px", "py")),
        check_vma=False,
    )
```
